128 devices in a mesh: row: 64 (over z, y, x), pan: 2 (over core).
Axes of the slice: x: 4, y: 4, z: 4, core: 2. Of those that a mesh axis runs over, the one named last changes fastest.
Arguments:
- right_side: float32 [256, 65536], P(None, 'row'), may hold values from -6 to 6
- initial_guess: float32 [256, 65536], P(None, ('row', 'pan')), may hold values from -6 to 6
- v_factor: float32 [128, 128, 16, 512], P('row', None, 'pan'), may hold values from -0.25 to 0.25
- u_factor: float32 [128, 128, 16, 512], P('row', None, 'pan'), may hold values from -0.125 to 0.125
- tile_ranks: int32 [128, 128], P(None, 'row'), may hold values from 0 to 16
- diag_block: float32 [65536, 512], P(('row', 'pan'))
- diag_inverse: float32 [65536, 512], P(('row', 'pan'))
Outputs:
- solution: float32 [256, 65536], P(None, ('row', 'pan'))
- residual: float32 [256, 65536], P(None, ('row', 'pan'))
The draws below stay inside these ranges and needn't reach their ends.
Inputs may be any that keep to these rules, and one draw needn't show every extreme that they name: `tile_ranks`: columns of a tile's factors from its rank on are ignored, as is the low-rank part of tile (i, i).
All inputs are finite; a program needn't handle non-finite values.
Results may differ from the reference program's by a relative error of at most 0.00017.
Values sent between devices are 32-bit elements; how exact they have to be, the bound alone decides.
A program may use at most 64 MiB of HBM per device.

```python
import jax
import jax.numpy as jnp
from jax import lax

B = 512
K = 16
NRHS = 256
ITERS = 2
NT = 128
ORDER = 65536


def draw_diag_block(key, part):
    first_key, second_key = jax.random.split(jax.random.fold_in(key, 11))
    row_pos = jnp.arange(NT * B, dtype=jnp.int32) % B
    col_pos = jnp.arange(B, dtype=jnp.int32)
    identity = (row_pos[:, None] == col_pos[None, :]).astype(jnp.float32)
    spread = jax.random.normal(first_key, (NT * B, B), jnp.float32)
    diagonal = jax.random.uniform(second_key, (NT * B, 1), jnp.float32, 2.0, 4.0)
    return spread * (1.0 / jnp.sqrt(jnp.float32(B))) * (1.0 - identity) + identity * diagonal


def draw_diag_inverse(key, part):
    first_key, second_key = jax.random.split(jax.random.fold_in(key, 23))
    row_pos = jnp.arange(NT * B, dtype=jnp.int32) % B
    col_pos = jnp.arange(B, dtype=jnp.int32)
    identity = (row_pos[:, None] == col_pos[None, :]).astype(jnp.float32)
    spread = jax.random.normal(first_key, (NT * B, B), jnp.float32)
    diagonal = jax.random.uniform(second_key, (NT * B, 1), jnp.float32, 0.2, 0.5)
    return spread * (0.15 / jnp.sqrt(jnp.float32(B))) * (1.0 - identity) + identity * diagonal


def touch_ends(values, own_key, smallest, largest):
    spot = [jax.random.randint(jax.random.fold_in(own_key, axis), (), 0, length) for axis, length in enumerate(values.shape)]
    main_axis = values.shape.index(max(values.shape))
    next_to = spot[:main_axis] + [(spot[main_axis] + 1) % values.shape[main_axis]] + spot[main_axis + 1:]
    return values.at[tuple(spot)].set(smallest).at[tuple(next_to)].set(largest)


def block_scale(rng, dims, cuts, low, high):
    def one(position, shards_of):
        steps = jax.random.uniform(jax.random.fold_in(jax.random.fold_in(rng, 6), position), (shards_of,), jnp.float32, low / len(cuts), high / len(cuts))
        return jnp.repeat(jnp.exp(steps), dims[position] // shards_of).reshape((-1,) + (1,) * (len(dims) - position - 1))

    loudness = one(*cuts[0])
    for cut in cuts[1:]:
        loudness = loudness * one(*cut)
    return loudness


def gaussian(own_key, dims, scale, bound, cuts=(), kind=jnp.bfloat16):
    result = scale * jax.random.normal(own_key, dims, jnp.float32)
    if cuts:
        result = result * block_scale(own_key, dims, cuts, -0.22, 0.18)
    return jnp.clip(result, -bound, bound).astype(kind)


def setup_inputs(seed: int = 0) -> dict:
    streams_of = jax.random.split(jax.random.key(seed), 8)
    return {
        "right_side": gaussian(streams_of[0], (NRHS, ORDER), 1.0, 6.0, ((1, 64),), jnp.float32),
        "initial_guess": gaussian(streams_of[1], (NRHS, ORDER), 1.0, 6.0, ((1, 128),), jnp.float32),
        "v_factor": gaussian(streams_of[2], (NT, NT, K, B), B ** -0.5, 0.25, ((0, 64), (2, 2)), jnp.float32),
        "u_factor": gaussian(streams_of[3], (NT, NT, K, B), (NT * K) ** -0.5, 0.125, ((0, 64), (2, 2)), jnp.float32),
        "tile_ranks": touch_ends(jax.random.randint(streams_of[4], (NT, NT), 0, K + 1), jax.random.fold_in(streams_of[4], 1), 0, K).astype(jnp.int32),
        "diag_block": draw_diag_block(jax.random.fold_in(streams_of[7], 71), 0),
        "diag_inverse": draw_diag_inverse(jax.random.fold_in(streams_of[7], 71), 0),
    }


def reference(right_side, initial_guess, v_factor, u_factor, tile_ranks, diag_block, diag_inverse):
    tile_count = tile_ranks.shape[0]
    tile_width = diag_block.shape[1]
    rank_cap = v_factor.shape[2]
    rhs_count = right_side.shape[0]
    components = jnp.arange(rank_cap, dtype=jnp.int32)
    tile_index = jnp.arange(tile_count, dtype=jnp.int32)
    off_diagonal = tile_index[:, None] != tile_index[None, :]
    rank_mask = ((components[None, None, :] < tile_ranks[:, :, None]) & off_diagonal[:, :, None]).astype(jnp.float32)
    block_rows = diag_block.reshape(tile_count, tile_width, tile_width)
    inverse_rows = diag_inverse.reshape(tile_count, tile_width, tile_width)
    highest = lax.Precision.HIGHEST

    def apply_matrix(guess):
        guess_tiles = guess.reshape(rhs_count, tile_count, tile_width)
        projected = jnp.einsum("jikb,rjb->ijkr", v_factor, guess_tiles, precision=highest)
        projected = projected * rank_mask[:, :, :, None]
        low_rank = jnp.einsum("ijkm,ijkr->rim", u_factor, projected, precision=highest)
        dense_part = jnp.einsum("imb,rib->rim", block_rows, guess_tiles, precision=highest)
        return (low_rank + dense_part).reshape(rhs_count, tile_count * tile_width)

    guess = initial_guess
    residual = right_side
    for iteration in range(ITERS):
        residual = right_side - apply_matrix(guess)
        residual_tiles = residual.reshape(rhs_count, tile_count, tile_width)
        update = jnp.einsum("imb,rib->rim", inverse_rows, residual_tiles, precision=highest)
        guess = guess + update.reshape(rhs_count, tile_count * tile_width)
    return guess, residual
```

```python
import jax
import jax.numpy as jnp
from jax import lax
from jax.experimental import pallas as pl
from jax.experimental.pallas import tpu as pltpu
from jax.sharding import PartitionSpec as P

MESH = pl.DeviceIdType.MESH
F32 = jnp.float32
BF16 = jnp.bfloat16
CHUNK = 128
MB = 512


def split(x):
    hi = x.astype(BF16)
    return hi, (x - hi.astype(F32)).astype(BF16)


def kernel(
    rhs_hbm, g_hbm, v_hbm, u_hbm, ranks, d_hbm, di_hbm, sol_hbm, res_hbm,
    gin, rin, vf, vh, vl, uf, uth, utl, df, dh, dl, dif, dih, dil,
    rhs, state, peer, dense, low, low_in, send, recv, wide, out_buf,
    load_sem, store_sem, send_sem, recv_sem, g_send, g_recv, l_send, l_recv,
):
    row = lax.axis_index("row")
    pan = lax.axis_index("pan")
    other = 1 - pan
    width = d_hbm.shape[0]
    z, y, x = row // 16, (row // 4) % 4, row % 4

    def shifted(a, b, c, sign):
        return (
            lax.rem(z + sign * (a + c) + 8, 4) * 16
            + lax.rem(y + sign * (a + b) + 8, 4) * 4
            + lax.rem(x + sign * a + 8, 4)
        )

    load_g = pltpu.make_async_copy(g_hbm, gin, load_sem.at[0])
    load_v = [
        pltpu.make_async_copy(v_hbm.at[c], vf.at[c], load_sem.at[1 + n])
        for n, c in enumerate((pan, other))
    ]
    load_u = pltpu.make_async_copy(u_hbm, uf, load_sem.at[3])
    load_d = pltpu.make_async_copy(d_hbm, df, load_sem.at[4])
    load_di = pltpu.make_async_copy(di_hbm, dif, load_sem.at[5])
    own_columns = pl.ds(pl.multiple_of(pan * width, width), width)
    load_r = pltpu.make_async_copy(rhs_hbm.at[:, own_columns], rin, load_sem.at[6])
    load_g.start()
    load_v[0].start()
    load_v[1].start()

    barrier = pltpu.get_barrier_semaphore()
    pl.semaphore_signal(barrier, inc=1, device_id=(row, other), device_id_type=MESH)

    def greet(n, carry):
        pl.semaphore_signal(
            barrier, inc=1, device_id=(lax.rem(row + n, 64), pan), device_id_type=MESH
        )
        return carry

    lax.fori_loop(1, 64, greet, 0)

    load_d.start()
    load_di.start()
    load_r.start()
    load_u.start()

    load_g.wait()
    for q in range(2):
        state[0, q] = gin[q * CHUNK:(q + 1) * CHUNK, :].T

    components = lax.broadcasted_iota(jnp.int32, (8, width), 0) + 8 * pan

    def prepare_v(c):
        def body(d, carry):
            tiles = []
            for e in range(2):
                i = 2 * d + e
                rank = jnp.where(i == 2 * row + c, 0, ranks[c, i])
                tiles.append(jnp.where(components < rank, vf[c, i], 0.0))
            hi, lo = split(jnp.concatenate(tiles, axis=0))
            rows = pl.ds(pl.multiple_of(16 * d, 16), 16)
            vh[c, rows, :] = hi
            vl[c, rows, :] = lo
            return carry

        lax.fori_loop(0, 64, body, 0, unroll=4)

    def product(ah, al, operand, start, size, depth):
        hi = operand[:, :CHUNK]
        both = jnp.dot(ah[start:start + size, :], operand[...], preferred_element_type=F32)
        return (
            both[:, :CHUNK] + both[:, CHUNK:]
            + jnp.dot(al[start:start + size, :], hi, preferred_element_type=F32)
        )

    def widen(target, value):
        hi, lo = split(value)
        target[:, :CHUNK] = hi
        target[:, CHUNK:] = lo

    def project(slot, c, value):
        operand = wide.at[pl.ds(0, width)]
        widen(operand, value)
        for start in range(0, 1024, MB):
            part = product(vh.at[c], vl.at[c], operand, start, MB, width)
            send[slot, start // 16:(start + MB) // 16, c] = part.reshape(MB // 16, 2, 8, CHUNK)

    def message(slot, n, target):
        return pltpu.make_async_remote_copy(
            src_ref=send.at[slot, target],
            dst_ref=recv.at[slot, n],
            send_sem=send_sem.at[slot],
            recv_sem=recv_sem.at[slot],
            device_id=(target, pan),
            device_id_type=MESH,
        )

    def all_messages(slot):
        return pltpu.make_async_remote_copy(
            src_ref=send.at[slot, pl.ds(1, 63)],
            dst_ref=recv.at[slot, pl.ds(1, 63)],
            send_sem=send_sem.at[slot],
            recv_sem=recv_sem.at[slot],
            device_id=(row, other),
            device_id_type=MESH,
        )

    def scatter(slot):
        for a in range(1, 4):
            message(slot, a, shifted(a, 0, 0, 1)).start()

        def body(m, carry):
            b, c = m % 4, m // 4
            for a in range(4):
                message(slot, 4 * m + a, shifted(a, b, c, 1)).start()
            return carry

        lax.fori_loop(1, 16, body, 0)
        recv[slot, 0] = send[slot, row]

    def to_peer(source, target, sems, recvs, n):
        return pltpu.make_async_remote_copy(
            src_ref=source,
            dst_ref=target,
            send_sem=sems.at[n],
            recv_sem=recvs.at[n],
            device_id=(row, other),
            device_id_type=MESH,
        )

    def guess_copy(it, q):
        return to_peer(state.at[it, q], peer.at[it, q], g_send, g_recv, 2 * it + q)

    def low_copy(slot):
        return to_peer(low.at[slot], low_in.at[slot], l_send, l_recv, slot)

    load_v[0].wait()
    prepare_v(pan)
    pl.semaphore_wait(barrier, 64)
    for q in range(2):
        guess_copy(0, q).start()
    project(0, pan, state[0, 0])
    load_v[1].wait()
    prepare_v(other)
    guess_copy(0, 0).wait_recv()
    project(0, other, peer[0, 0])
    scatter(0)
    project(1, pan, state[0, 1])
    guess_copy(0, 1).wait_recv()
    project(1, other, peer[0, 1])
    scatter(1)

    load_u.wait()
    for i in range(2):
        def turn(m, carry):
            pieces = []
            for n in range(8):
                order = 8 * m + n
                a, b, c = order % 4, (order // 4) % 4, order // 16
                source = shifted(a, b, c, -1)
                for e in range(2):
                    pieces.append(uf[i, 2 * source + e])
            hi, lo = split(jnp.concatenate(pieces, axis=0).T)
            columns = pl.ds(pl.multiple_of(128 * m, 128), 128)
            uth[i, :, columns] = hi
            utl[i, :, columns] = lo
            return carry

        lax.fori_loop(0, 8, turn, 0)
    load_d.wait()
    dh[...], dl[...] = split(df[...])
    load_di.wait()
    dih[...], dil[...] = split(dif[...])
    load_r.wait()

    def subtract_dense(it, q):
        operand = wide.at[pl.ds(0, width)]
        widen(operand, state[it, q])
        dense[q] = rhs[q] - product(dh, dl, operand, 0, width, width)

    for q in range(2):
        rhs[q] = rin[q * CHUNK:(q + 1) * CHUNK, :].T
        subtract_dense(0, q)

    def low_rank(slot, i):
        widen(wide, recv[slot, :, :, i].reshape(1024, CHUNK))
        return product(uth.at[i], utl.at[i], wide, 0, width, 1024)

    def advance(it, q):
        slot = 2 * it + q
        all_messages(slot).wait_recv()
        low[slot] = low_rank(slot, other)
        low_copy(slot).start()
        own = low_rank(slot, pan)
        low_copy(slot).wait_recv()
        residual = dense[q] - (own + low_in[slot])
        operand = wide.at[pl.ds(0, width)]
        widen(operand, residual)
        update = product(dih, dil, operand, 0, width, width)
        return residual, state[it, q] + update

    for q in range(2):
        residual, guess = advance(0, q)
        state[1, q] = guess
        guess_copy(1, q).start()
        project(2 + q, pan, guess)
        guess_copy(1, q).wait_recv()
        project(2 + q, other, peer[1, q])
        scatter(2 + q)
        subtract_dense(1, q)

    stores = []
    for q in range(2):
        residual, guess = advance(1, q)
        out_buf[0, q] = residual.T
        out_buf[1, q] = guess.T
        for n, target in enumerate((res_hbm, sol_hbm)):
            store = pltpu.make_async_copy(
                out_buf.at[n, q], target.at[pl.ds(q * CHUNK, CHUNK)], store_sem.at[2 * n + q]
            )
            store.start()
            stores.append(store)

    for slot in range(4):
        all_messages(slot).wait_send()
        low_copy(slot).wait_send()
        guess_copy(slot // 2, slot % 2).wait_send()
    for store in stores:
        store.wait()


def on_device(right_side, initial_guess, v_factor, u_factor, tile_ranks, diag_block, diag_inverse):
    any_space = pl.BlockSpec(memory_space=pl.ANY)
    tiles, count, part, width = v_factor.shape
    rhs_count = initial_guess.shape[0]
    shape = jax.ShapeDtypeStruct(initial_guess.shape, F32)
    sol, res = pl.pallas_call(
        kernel,
        name="richardson",
        out_shape=(shape, shape),
        in_specs=[any_space] * 4 + [pl.BlockSpec(memory_space=pltpu.SMEM)] + [any_space] * 2,
        out_specs=(any_space, any_space),
        scratch_shapes=[
            pltpu.VMEM((rhs_count, width), F32),
            pltpu.VMEM((rhs_count, width), F32),
            pltpu.VMEM((tiles, count, part, width), F32),
            pltpu.VMEM((tiles, count * part, width), BF16),
            pltpu.VMEM((tiles, count * part, width), BF16),
            pltpu.VMEM((tiles, count, part, width), F32),
            pltpu.VMEM((tiles, width, count * part), BF16),
            pltpu.VMEM((tiles, width, count * part), BF16),
            pltpu.VMEM((width, width), F32),
            pltpu.VMEM((width, width), BF16),
            pltpu.VMEM((width, width), BF16),
            pltpu.VMEM((width, width), F32),
            pltpu.VMEM((width, width), BF16),
            pltpu.VMEM((width, width), BF16),
            pltpu.VMEM((2, width, CHUNK), F32),
            pltpu.VMEM((2, 2, width, CHUNK), F32),
            pltpu.VMEM((2, 2, width, CHUNK), F32),
            pltpu.VMEM((2, width, CHUNK), F32),
            pltpu.VMEM((4, width, CHUNK), F32),
            pltpu.VMEM((4, width, CHUNK), F32),
            pltpu.VMEM((4, 64, tiles, tiles, part, CHUNK), F32),
            pltpu.VMEM((4, 64, tiles, tiles, part, CHUNK), F32),
            pltpu.VMEM((1024, 2 * CHUNK), BF16),
            pltpu.VMEM((2, 2, CHUNK, width), F32),
            pltpu.SemaphoreType.DMA((7,)),
            pltpu.SemaphoreType.DMA((4,)),
            pltpu.SemaphoreType.DMA((4,)),
            pltpu.SemaphoreType.DMA((4,)),
            pltpu.SemaphoreType.DMA((4,)),
            pltpu.SemaphoreType.DMA((4,)),
            pltpu.SemaphoreType.DMA((4,)),
            pltpu.SemaphoreType.DMA((4,)),
        ],
        compiler_params=pltpu.CompilerParams(
            collective_id=0, has_side_effects=True, vmem_limit_bytes=56 << 20
        ),
    )(right_side, initial_guess, v_factor, u_factor, tile_ranks.T, diag_block, diag_inverse)
    return sol, res


def solution(mesh):
    placed = (
        P(None, "row"),
        P(None, ("row", "pan")),
        P("row", None, "pan", None),
        P("row", None, "pan", None),
        P(None, "row"),
        P(("row", "pan"), None),
        P(("row", "pan"), None),
    )
    return jax.shard_map(
        on_device,
        mesh=mesh,
        in_specs=placed,
        out_specs=(P(None, ("row", "pan")), P(None, ("row", "pan"))),
        check_vma=False,
    )
```

```python
import jax
import jax.numpy as jnp
from jax import lax
from jax.experimental import pallas as pl
from jax.experimental.pallas import tpu as pltpu
from jax.sharding import PartitionSpec as P

MESH = pl.DeviceIdType.MESH
F32 = jnp.float32
BF16 = jnp.bfloat16
CHUNK = 128
MB = 512


def split(x):
    hi = x.astype(BF16)
    return hi, (x - hi.astype(F32)).astype(BF16)


def kernel(
    rhs_hbm, g_hbm, v_hbm, u_hbm, ranks, d_hbm, di_hbm, result,
    gin, rin, vf, vh, vl, uf, uth, utl, df, dh, dl, dif, dih, dil,
    rhs, state, peer, dense, low, low_in, send, recv, wide,
    load_sem, send_sem, recv_sem, g_send, g_recv, l_send, l_recv,
):
    row = lax.axis_index("row")
    pan = lax.axis_index("pan")
    other = 1 - pan
    width = d_hbm.shape[0]
    z, y, x = row // 16, (row // 4) % 4, row % 4

    def shifted(a, b, c, sign):
        return (
            lax.rem(z - sign * (a + b) + 8, 4) * 16
            + lax.rem(y + sign * (a + 2 * b + c) + 16, 4) * 4
            + lax.rem(x + sign * a + 8, 4)
        )

    load_g = pltpu.make_async_copy(g_hbm, gin, load_sem.at[0])
    load_v = [
        pltpu.make_async_copy(v_hbm.at[c], vf.at[c], load_sem.at[1 + n])
        for n, c in enumerate((pan, other))
    ]
    load_u = pltpu.make_async_copy(u_hbm, uf, load_sem.at[3])
    load_d = pltpu.make_async_copy(d_hbm, df, load_sem.at[4])
    load_di = pltpu.make_async_copy(di_hbm, dif, load_sem.at[5])
    own_columns = pl.ds(pl.multiple_of(pan * width, width), width)
    load_r = pltpu.make_async_copy(rhs_hbm.at[:, own_columns], rin, load_sem.at[6])
    load_g.start()
    load_v[0].start()
    load_v[1].start()

    barrier = pltpu.get_barrier_semaphore()
    pl.semaphore_signal(barrier, inc=1, device_id=(row, other), device_id_type=MESH)

    def greet(n, carry):
        pl.semaphore_signal(
            barrier, inc=1, device_id=(lax.rem(row + n, 64), pan), device_id_type=MESH
        )
        return carry

    lax.fori_loop(1, 64, greet, 0)

    load_d.start()
    load_di.start()
    load_r.start()
    load_u.start()

    load_g.wait()
    for q in range(2):
        state[0, q] = gin[q * CHUNK:(q + 1) * CHUNK, :].T

    components = lax.broadcasted_iota(jnp.int32, (8, width), 0) + 8 * pan

    def prepare_v(c, d):
        tiles = []
        for e in range(2):
            i = 2 * d + e
            rank = jnp.where(i == 2 * row + c, 0, ranks[c, i])
            tiles.append(jnp.where(components < rank, vf[c, i], 0.0))
        hi, lo = split(jnp.concatenate(tiles, axis=0))
        rows = pl.ds(pl.multiple_of(16 * d, 16), 16)
        vh[c, rows, :] = hi
        vl[c, rows, :] = lo

    def product(ah, al, operand, start, size, depth):
        hi = operand[:, :CHUNK]
        both = jnp.dot(ah[start:start + size, :], operand[...], preferred_element_type=F32)
        return (
            both[:, :CHUNK] + both[:, CHUNK:]
            + jnp.dot(al[start:start + size, :], hi, preferred_element_type=F32)
        )

    def widen(target, value):
        hi, lo = split(value)
        target[:, :CHUNK] = hi
        target[:, CHUNK:] = lo

    def project(slot, c, value):
        operand = wide.at[pl.ds(0, width)]
        widen(operand, value)
        for start in range(0, 1024, MB):
            part = product(vh.at[c], vl.at[c], operand, start, MB, width)
            send[slot, start // 16:(start + MB) // 16, c] = part.reshape(MB // 16, 2, 8, CHUNK)

    def message(slot, n, target):
        return pltpu.make_async_remote_copy(
            src_ref=send.at[slot, target],
            dst_ref=recv.at[slot, n],
            send_sem=send_sem.at[slot],
            recv_sem=recv_sem.at[slot],
            device_id=(target, pan),
            device_id_type=MESH,
        )

    def all_messages(slot):
        return pltpu.make_async_remote_copy(
            src_ref=send.at[slot, pl.ds(1, 63)],
            dst_ref=recv.at[slot, pl.ds(1, 63)],
            send_sem=send_sem.at[slot],
            recv_sem=recv_sem.at[slot],
            device_id=(row, other),
            device_id_type=MESH,
        )

    def half_message(slot, n, target, c):
        return pltpu.make_async_remote_copy(
            src_ref=send.at[slot, target, c],
            dst_ref=recv.at[slot, n, c],
            send_sem=send_sem.at[slot],
            recv_sem=recv_sem.at[slot],
            device_id=(target, pan),
            device_id_type=MESH,
        )

    def in_order(visit):
        for a in range(4):
            visit(a, a, 0, 0)

        def body(m, carry):
            b, c = m % 4, m // 4
            for a in range(4):
                visit(4 * m + a, a, b, c)
            return carry

        lax.fori_loop(1, 16, body, 0)

    def scatter(slot):
        def visit(n, a, b, c):
            if not (isinstance(n, int) and n == 0):
                message(slot, n, shifted(a, b, c, 1)).start()

        in_order(visit)
        recv[slot, 0] = send[slot, row]

    def scatter_half(slot, part, beside=None):
        def visit(n, a, b, c):
            if not (isinstance(n, int) and n == 0):
                half_message(slot, n, shifted(a, b, c, 1), part).start()
            if beside is not None:
                beside(n)

        in_order(visit)
        recv[slot, 0, part] = send[slot, row, part]

    def to_peer(source, target, sems, recvs, n):
        return pltpu.make_async_remote_copy(
            src_ref=source,
            dst_ref=target,
            send_sem=sems.at[n],
            recv_sem=recvs.at[n],
            device_id=(row, other),
            device_id_type=MESH,
        )

    def guess_copy(it, q):
        return to_peer(state.at[it, q], peer.at[it, q], g_send, g_recv, 2 * it + q)

    def low_copy(slot):
        return to_peer(low.at[slot], low_in.at[slot], l_send, l_recv, slot)

    load_v[0].wait()

    def prepare_own(d, carry):
        prepare_v(pan, d)
        return carry

    lax.fori_loop(0, 64, prepare_own, 0, unroll=4)
    project(0, pan, state[0, 0])
    pl.semaphore_wait(barrier, 64)
    for q in range(2):
        guess_copy(0, q).start()
    load_v[1].wait()
    scatter_half(0, pan, lambda d: prepare_v(other, d))
    guess_copy(0, 0).wait_recv()
    project(0, other, peer[0, 0])
    scatter_half(0, other)
    project(1, pan, state[0, 1])
    guess_copy(0, 1).wait_recv()
    project(1, other, peer[0, 1])
    scatter(1)

    load_u.wait()
    for i in range(2):
        def turn(m, carry):
            pieces = []
            for n in range(8):
                order = 8 * m + n
                a, b, c = order % 4, (order // 4) % 4, order // 16
                source = shifted(a, b, c, -1)
                for e in range(2):
                    pieces.append(uf[i, 2 * source + e])
            hi, lo = split(jnp.concatenate(pieces, axis=0).T)
            columns = pl.ds(pl.multiple_of(128 * m, 128), 128)
            uth[i, :, columns] = hi
            utl[i, :, columns] = lo
            return carry

        lax.fori_loop(0, 8, turn, 0)
    load_d.wait()
    dh[...], dl[...] = split(df[...])
    load_di.wait()
    dih[...], dil[...] = split(dif[...])
    load_r.wait()

    def subtract_dense(it, q):
        operand = wide.at[pl.ds(0, width)]
        widen(operand, state[it, q])
        dense[q] = rhs[q] - product(dh, dl, operand, 0, width, width)

    for q in range(2):
        rhs[q] = rin[q * CHUNK:(q + 1) * CHUNK, :].T
        subtract_dense(0, q)

    def low_rank(slot, i):
        widen(wide, recv[slot, :, :, i].reshape(1024, CHUNK))
        return product(uth.at[i], utl.at[i], wide, 0, width, 1024)

    def advance(it, q):
        slot = 2 * it + q
        all_messages(slot).wait_recv()
        low[slot] = low_rank(slot, other)
        low_copy(slot).start()
        own = low_rank(slot, pan)
        low_copy(slot).wait_recv()
        residual = dense[q] - (own + low_in[slot])
        operand = wide.at[pl.ds(0, width)]
        widen(operand, residual)
        update = product(dih, dil, operand, 0, width, width)
        return residual, state[it, q] + update

    for q in range(2):
        residual, guess = advance(0, q)
        state[1, q] = guess
        guess_copy(1, q).start()
        project(2 + q, pan, guess)
        guess_copy(1, q).wait_recv()
        project(2 + q, other, peer[1, q])
        scatter(2 + q)
        subtract_dense(1, q)

    for q in range(2):
        residual, guess = advance(1, q)
        result[0, q] = guess
        result[1, q] = residual

    for slot in range(4):
        all_messages(slot).wait_send()
        low_copy(slot).wait_send()
        guess_copy(slot // 2, slot % 2).wait_send()

def finish(result, sol_hbm, res_hbm, out_buf, store_sem):
    stores = []
    for q in range(2):
        for n, target in enumerate((sol_hbm, res_hbm)):
            out_buf[n, q] = result[n, q].T
            store = pltpu.make_async_copy(
                out_buf.at[n, q], target.at[pl.ds(q * CHUNK, CHUNK)], store_sem.at[2 * n + q]
            )
            store.start()
            stores.append(store)
    for store in stores:
        store.wait()


def on_device(right_side, initial_guess, v_factor, u_factor, tile_ranks, diag_block, diag_inverse):
    any_space = pl.BlockSpec(memory_space=pl.ANY)
    tiles, count, part, width = v_factor.shape
    rhs_count = initial_guess.shape[0]
    shape = jax.ShapeDtypeStruct(initial_guess.shape, F32)
    result = pl.pallas_call(
        kernel,
        name="richardson",
        out_shape=pltpu.VMEM((2, 2, width, CHUNK), F32),
        in_specs=[any_space] * 4 + [pl.BlockSpec(memory_space=pltpu.SMEM)] + [any_space] * 2,
        out_specs=pl.BlockSpec(memory_space=pltpu.VMEM),
        scratch_shapes=[
            pltpu.VMEM((rhs_count, width), F32),
            pltpu.VMEM((rhs_count, width), F32),
            pltpu.VMEM((tiles, count, part, width), F32),
            pltpu.VMEM((tiles, count * part, width), BF16),
            pltpu.VMEM((tiles, count * part, width), BF16),
            pltpu.VMEM((tiles, count, part, width), F32),
            pltpu.VMEM((tiles, width, count * part), BF16),
            pltpu.VMEM((tiles, width, count * part), BF16),
            pltpu.VMEM((width, width), F32),
            pltpu.VMEM((width, width), BF16),
            pltpu.VMEM((width, width), BF16),
            pltpu.VMEM((width, width), F32),
            pltpu.VMEM((width, width), BF16),
            pltpu.VMEM((width, width), BF16),
            pltpu.VMEM((2, width, CHUNK), F32),
            pltpu.VMEM((2, 2, width, CHUNK), F32),
            pltpu.VMEM((2, 2, width, CHUNK), F32),
            pltpu.VMEM((2, width, CHUNK), F32),
            pltpu.VMEM((4, width, CHUNK), F32),
            pltpu.VMEM((4, width, CHUNK), F32),
            pltpu.VMEM((4, 64, tiles, tiles, part, CHUNK), F32),
            pltpu.VMEM((4, 64, tiles, tiles, part, CHUNK), F32),
            pltpu.VMEM((1024, 2 * CHUNK), BF16),
            pltpu.SemaphoreType.DMA((7,)),
            pltpu.SemaphoreType.DMA((4,)),
            pltpu.SemaphoreType.DMA((4,)),
            pltpu.SemaphoreType.DMA((4,)),
            pltpu.SemaphoreType.DMA((4,)),
            pltpu.SemaphoreType.DMA((4,)),
            pltpu.SemaphoreType.DMA((4,)),
        ],
        compiler_params=pltpu.CompilerParams(
            collective_id=0, has_side_effects=True, vmem_limit_bytes=58 << 20
        ),
    )(right_side, initial_guess, v_factor, u_factor, tile_ranks.T, diag_block, diag_inverse)
    return pl.pallas_call(
        finish,
        name="finish",
        out_shape=(shape, shape),
        in_specs=[pl.BlockSpec(memory_space=pltpu.VMEM)],
        out_specs=(any_space, any_space),
        scratch_shapes=[
            pltpu.VMEM((2, 2, CHUNK, width), F32),
            pltpu.SemaphoreType.DMA((4,)),
        ],
        compiler_params=pltpu.CompilerParams(vmem_limit_bytes=8 << 20),
    )(result)


def solution(mesh):
    placed = (
        P(None, "row"),
        P(None, ("row", "pan")),
        P("row", None, "pan", None),
        P("row", None, "pan", None),
        P(None, "row"),
        P(("row", "pan"), None),
        P(("row", "pan"), None),
    )
    return jax.shard_map(
        on_device,
        mesh=mesh,
        in_specs=placed,
        out_specs=(P(None, ("row", "pan")), P(None, ("row", "pan"))),
        check_vma=False,
    )
```

```python
import jax
import jax.numpy as jnp
from jax import lax
from jax.experimental import pallas as pl
from jax.experimental.pallas import tpu as pltpu
from jax.sharding import PartitionSpec as P

MESH = pl.DeviceIdType.MESH
F32 = jnp.float32
BF16 = jnp.bfloat16
CHUNK = 128
MB = 1024
EARLY = 40


SHIFTS = [(-(a + b) % 4, (a + 2 * b + c) % 4, a) for c in range(4) for b in range(4) for a in range(4)]


def split(x):
    hi = x.astype(BF16)
    return hi, (x - hi.astype(F32)).astype(BF16)


def kernel(
    rhs_hbm, g_hbm, v_hbm, u_hbm, ranks_hbm, d_hbm, di_hbm, result,
    gin, rin, vf, vh, vl, uf, uth, utl, df, dh, dl, dif, dih, dil,
    rhs, state, peer, dense, low, low_in, part, send, recv, wide,
    ranks, targets, sources, load_sem, send_sem, recv_sem, g_send, g_recv, l_send, l_recv,
):
    row = lax.axis_index("row")
    pan = lax.axis_index("pan")
    other = 1 - pan
    width = d_hbm.shape[0]
    z, y, x = row // 16, (row // 4) % 4, row % 4

    def shifted(n, sign):
        dz, dy, dx = SHIFTS[n]
        return (
            lax.rem(z + sign * dz + 4, 4) * 16
            + lax.rem(y + sign * dy + 4, 4) * 4
            + lax.rem(x + sign * dx + 4, 4)
        )

    load_g = pltpu.make_async_copy(g_hbm, gin, load_sem.at[0])
    load_v = [
        pltpu.make_async_copy(v_hbm.at[c], vf.at[c], load_sem.at[1 + n])
        for n, c in enumerate((pan, other))
    ]
    load_u = pltpu.make_async_copy(u_hbm, uf, load_sem.at[3])
    load_d = pltpu.make_async_copy(d_hbm, df, load_sem.at[4])
    load_di = pltpu.make_async_copy(di_hbm, dif, load_sem.at[5])
    own_columns = pl.ds(pl.multiple_of(pan * width, width), width)
    load_r = pltpu.make_async_copy(rhs_hbm.at[:, own_columns], rin, load_sem.at[6])
    load_ranks = pltpu.make_async_copy(ranks_hbm, ranks, load_sem.at[7])
    load_g.start()
    load_v[0].start()

    barrier = pltpu.get_barrier_semaphore()
    pl.semaphore_signal(barrier, inc=1, device_id=(row, other), device_id_type=MESH)

    def greet(n, carry):
        pl.semaphore_signal(
            barrier, inc=1, device_id=(lax.rem(row + n, 64), pan), device_id_type=MESH
        )
        return carry

    lax.fori_loop(1, 64, greet, 0, unroll=9)
    load_ranks.start()
    load_v[1].start()
    for n in range(1, 64):
        targets[n] = shifted(n, 1)

    load_g.wait()
    for q in range(2):
        state[0, q] = gin[q * CHUNK:(q + 1) * CHUNK, :].T

    components = lax.broadcasted_iota(jnp.int32, (8, width), 0) + 8 * pan

    def prepare_v(c, d):
        tiles = []
        for e in range(2):
            i = 2 * d + e
            rank = jnp.where(i == 2 * row + c, 0, ranks[c, i])
            tiles.append(jnp.where(components < rank, vf[c, i], 0.0))
        hi, lo = split(jnp.concatenate(tiles, axis=0))
        rows = pl.ds(pl.multiple_of(16 * d, 16), 16)
        vh[c, rows, :] = hi
        vl[c, rows, :] = lo

    def product(ah, al, operand):
        both = jnp.dot(ah[...], operand[...], preferred_element_type=F32)
        return (
            both[:, :CHUNK] + both[:, CHUNK:]
            + jnp.dot(al[...], operand[:, :CHUNK], preferred_element_type=F32)
        )

    def widen(target, value):
        hi, lo = split(value)
        target[:, :CHUNK] = hi
        target[:, CHUNK:] = lo

    def project(slot, c, value):
        operand = wide.at[pl.ds(0, width)]
        widen(operand, value)
        for start in range(0, 1024, MB):
            rows = pl.ds(start, MB)
            block = product(vh.at[c, rows], vl.at[c, rows], operand)
            send[slot, start // 16:(start + MB) // 16, c] = block.reshape(MB // 16, 2, 8, CHUNK)

    def message(slot, n, target):
        return pltpu.make_async_remote_copy(
            src_ref=send.at[slot, target],
            dst_ref=recv.at[slot, n],
            send_sem=send_sem.at[slot],
            recv_sem=recv_sem.at[slot, n // EARLY],
            device_id=(target, pan),
            device_id_type=MESH,
        )

    def all_messages(slot, late):
        first, count = (EARLY, 64 - EARLY) if late else (1, EARLY - 1)
        return pltpu.make_async_remote_copy(
            src_ref=send.at[slot, pl.ds(first, count)],
            dst_ref=recv.at[slot, pl.ds(first, count)],
            send_sem=send_sem.at[slot],
            recv_sem=recv_sem.at[slot, late],
            device_id=(row, other),
            device_id_type=MESH,
        )

    def half_message(slot, n, target, c):
        return pltpu.make_async_remote_copy(
            src_ref=send.at[slot, target, c],
            dst_ref=recv.at[slot, n, c],
            send_sem=send_sem.at[slot],
            recv_sem=recv_sem.at[slot, n // EARLY],
            device_id=(target, pan),
            device_id_type=MESH,
        )

    def in_order(visit):
        for n in range(1, 4):
            visit(n)

        def body(m, carry):
            for n in range(4):
                visit(4 * m + n)
            return carry

        lax.fori_loop(1, 16, body, 0)

    def scatter(slot):
        in_order(lambda n: message(slot, n, targets[n]).start())
        recv[slot, 0] = send[slot, row]

    def scatter_half(slot, tile, beside=None):
        def visit(n):
            half_message(slot, n, targets[n], tile).start()
            if beside is not None:
                beside(n)

        if beside is not None:
            beside(0)
        in_order(visit)
        recv[slot, 0, tile] = send[slot, row, tile]

    def to_peer(source, target, sems, recvs, n):
        return pltpu.make_async_remote_copy(
            src_ref=source,
            dst_ref=target,
            send_sem=sems.at[n],
            recv_sem=recvs.at[n],
            device_id=(row, other),
            device_id_type=MESH,
        )

    def guess_copy(it, q):
        return to_peer(state.at[it, q], peer.at[it, q], g_send, g_recv, 2 * it + q)

    def low_copy(slot):
        return to_peer(low.at[slot], low_in.at[slot], l_send, l_recv, slot)

    load_v[0].wait()
    load_ranks.wait()

    def prepare_own(d, carry):
        prepare_v(pan, d)
        return carry

    lax.fori_loop(0, 64, prepare_own, 0, unroll=4)
    project(0, pan, state[0, 0])
    pl.semaphore_wait(barrier, 64)
    for q in range(2):
        guess_copy(0, q).start()
    load_v[1].wait()
    for load in (load_d, load_di, load_r, load_u):
        load.start()
    scatter_half(0, pan, lambda d: prepare_v(other, d))
    guess_copy(0, 0).wait_recv()
    project(0, other, peer[0, 0])
    scatter_half(0, other)
    project(1, pan, state[0, 1])
    guess_copy(0, 1).wait_recv()
    project(1, other, peer[0, 1])
    scatter(1)

    for n in range(64):
        sources[n] = shifted(n, -1)
    load_u.wait()
    for i in range(2):
        def turn(m, carry):
            pieces = []
            for n in range(8):
                source = sources[8 * m + n]
                for e in range(2):
                    pieces.append(uf[i, 2 * source + e])
            hi, lo = split(jnp.concatenate(pieces, axis=0).T)
            columns = pl.ds(pl.multiple_of(128 * m, 128), 128)
            uth[i, :, columns] = hi
            utl[i, :, columns] = lo
            return carry

        lax.fori_loop(0, 8, turn, 0)
    load_d.wait()
    dh[...], dl[...] = split(df[...])
    load_di.wait()
    dih[...], dil[...] = split(dif[...])
    load_r.wait()

    def subtract_dense(it, q):
        operand = wide.at[pl.ds(0, width)]
        widen(operand, state[it, q])
        dense[q] = rhs[q] - product(dh, dl, operand)

    for q in range(2):
        rhs[q] = rin[q * CHUNK:(q + 1) * CHUNK, :].T
        subtract_dense(0, q)

    def low_rank(slot, i, late):
        first, count = (EARLY, 64 - EARLY) if late else (0, EARLY)
        columns = pl.ds(16 * first, 16 * count)
        operand = wide.at[columns]
        widen(operand, recv[slot, first:first + count, :, i].reshape(16 * count, CHUNK))
        return product(uth.at[i, :, columns], utl.at[i, :, columns], operand)

    def advance(it, q):
        slot = 2 * it + q
        all_messages(slot, 0).wait_recv()
        part[0] = low_rank(slot, other, 0)
        part[1] = low_rank(slot, pan, 0)
        all_messages(slot, 1).wait_recv()
        low[slot] = part[0] + low_rank(slot, other, 1)
        low_copy(slot).start()
        own = dense[q] - (part[1] + low_rank(slot, pan, 1))
        low_copy(slot).wait_recv()
        residual = own - low_in[slot]
        operand = wide.at[pl.ds(0, width)]
        widen(operand, residual)
        return residual, state[it, q] + product(dih, dil, operand)

    for q in range(2):
        residual, guess = advance(0, q)
        state[1, q] = guess
        guess_copy(1, q).start()
        project(2 + q, pan, guess)
        guess_copy(1, q).wait_recv()
        project(2 + q, other, peer[1, q])
        scatter(2 + q)
        subtract_dense(1, q)

    for q in range(2):
        residual, guess = advance(1, q)
        result[0, q * CHUNK:(q + 1) * CHUNK] = guess.T
        result[1, q * CHUNK:(q + 1) * CHUNK] = residual.T

    for slot in range(4):
        for late in range(2):
            all_messages(slot, late).wait_send()
        low_copy(slot).wait_send()
        guess_copy(slot // 2, slot % 2).wait_send()

def finish(result, sol_hbm, res_hbm, store_sem):
    stores = [
        pltpu.make_async_copy(result.at[n], target, store_sem.at[n])
        for n, target in enumerate((sol_hbm, res_hbm))
    ]
    for store in stores:
        store.start()
    for store in stores:
        store.wait()


def on_device(right_side, initial_guess, v_factor, u_factor, tile_ranks, diag_block, diag_inverse):
    any_space = pl.BlockSpec(memory_space=pl.ANY)
    tiles, count, part, width = v_factor.shape
    rhs_count = initial_guess.shape[0]
    shape = jax.ShapeDtypeStruct(initial_guess.shape, F32)
    result = pl.pallas_call(
        kernel,
        name="richardson",
        out_shape=pltpu.VMEM((2, rhs_count, width), F32),
        in_specs=[any_space] * 7,
        out_specs=pl.BlockSpec(memory_space=pltpu.VMEM),
        scratch_shapes=[
            pltpu.VMEM((rhs_count, width), F32),
            pltpu.VMEM((rhs_count, width), F32),
            pltpu.VMEM((tiles, count, part, width), F32),
            pltpu.VMEM((tiles, count * part, width), BF16),
            pltpu.VMEM((tiles, count * part, width), BF16),
            pltpu.VMEM((tiles, count, part, width), F32),
            pltpu.VMEM((tiles, width, count * part), BF16),
            pltpu.VMEM((tiles, width, count * part), BF16),
            pltpu.VMEM((width, width), F32),
            pltpu.VMEM((width, width), BF16),
            pltpu.VMEM((width, width), BF16),
            pltpu.VMEM((width, width), F32),
            pltpu.VMEM((width, width), BF16),
            pltpu.VMEM((width, width), BF16),
            pltpu.VMEM((2, width, CHUNK), F32),
            pltpu.VMEM((2, 2, width, CHUNK), F32),
            pltpu.VMEM((2, 2, width, CHUNK), F32),
            pltpu.VMEM((2, width, CHUNK), F32),
            pltpu.VMEM((4, width, CHUNK), F32),
            pltpu.VMEM((4, width, CHUNK), F32),
            pltpu.VMEM((2, width, CHUNK), F32),
            pltpu.VMEM((4, 64, tiles, tiles, part, CHUNK), F32),
            pltpu.VMEM((4, 64, tiles, tiles, part, CHUNK), F32),
            pltpu.VMEM((1024, 2 * CHUNK), BF16),
            pltpu.SMEM(tile_ranks.shape[::-1], jnp.int32),
            pltpu.SMEM((64,), jnp.int32),
            pltpu.SMEM((64,), jnp.int32),
            pltpu.SemaphoreType.DMA((8,)),
            pltpu.SemaphoreType.DMA((4,)),
            pltpu.SemaphoreType.DMA((4, 2)),
            pltpu.SemaphoreType.DMA((4,)),
            pltpu.SemaphoreType.DMA((4,)),
            pltpu.SemaphoreType.DMA((4,)),
            pltpu.SemaphoreType.DMA((4,)),
        ],
        compiler_params=pltpu.CompilerParams(
            collective_id=0, has_side_effects=True, vmem_limit_bytes=58 << 20
        ),
    )(right_side, initial_guess, v_factor, u_factor, tile_ranks.T, diag_block, diag_inverse)
    return pl.pallas_call(
        finish,
        name="finish",
        out_shape=(shape, shape),
        in_specs=[pl.BlockSpec(memory_space=pltpu.VMEM)],
        out_specs=(any_space, any_space),
        scratch_shapes=[pltpu.SemaphoreType.DMA((2,))],
        compiler_params=pltpu.CompilerParams(vmem_limit_bytes=8 << 20),
    )(result)


def solution(mesh):
    placed = (
        P(None, "row"),
        P(None, ("row", "pan")),
        P("row", None, "pan", None),
        P("row", None, "pan", None),
        P(None, "row"),
        P(("row", "pan"), None),
        P(("row", "pan"), None),
    )
    return jax.shard_map(
        on_device,
        mesh=mesh,
        in_specs=placed,
        out_specs=(P(None, ("row", "pan")), P(None, ("row", "pan"))),
        check_vma=False,
    )
```

```python
import jax
import jax.numpy as jnp
from jax import lax
from jax.experimental import pallas as pl
from jax.experimental.pallas import tpu as pltpu
from jax.sharding import PartitionSpec as P

MESH = pl.DeviceIdType.MESH
F32 = jnp.float32
BF16 = jnp.bfloat16
CHUNK = 128
MB = 1024
EARLY = 40
SHARED = 32
LATE = 64 - SHARED


SHIFTS = [(-(a + b) % 4, (a + 2 * b + c) % 4, a) for c in range(4) for b in range(4) for a in range(4)]


def split(x):
    hi = x.astype(BF16)
    return hi, (x - hi.astype(F32)).astype(BF16)


def kernel(
    rhs_hbm, g_hbm, v_hbm, u_hbm, ranks_hbm, d_hbm, di_hbm, result,
    gin, rin, vf, vh, vl, uf, uth, utl, df, dh, dl, dif, dih, dil,
    rhs, state, peer, dense, low, low_in, part, send, recv, wide, uf_peer, uth_peer, utl_peer, recv_last,
    ranks, targets, sources, load_sem, send_sem, recv_sem, g_send, g_recv, l_send, l_recv, u_send, u_recv, last_recv,
):
    row = lax.axis_index("row")
    pan = lax.axis_index("pan")
    other = 1 - pan
    width = d_hbm.shape[0]
    z, y, x = row // 16, (row // 4) % 4, row % 4

    def shifted(n, sign):
        dz, dy, dx = SHIFTS[n]
        return (
            lax.rem(z + sign * dz + 4, 4) * 16
            + lax.rem(y + sign * dy + 4, 4) * 4
            + lax.rem(x + sign * dx + 4, 4)
        )

    load_g = pltpu.make_async_copy(g_hbm, gin, load_sem.at[0])
    load_v = [
        pltpu.make_async_copy(v_hbm.at[c], vf.at[c], load_sem.at[1 + n])
        for n, c in enumerate((pan, other))
    ]
    load_u = pltpu.make_async_copy(u_hbm, uf, load_sem.at[3])
    load_d = pltpu.make_async_copy(d_hbm, df, load_sem.at[4])
    load_di = pltpu.make_async_copy(di_hbm, dif, load_sem.at[5])
    own_columns = pl.ds(pl.multiple_of(pan * width, width), width)
    load_r = pltpu.make_async_copy(rhs_hbm.at[:, own_columns], rin, load_sem.at[6])
    load_ranks = pltpu.make_async_copy(ranks_hbm, ranks, load_sem.at[7])
    load_g.start()
    load_v[0].start()

    barrier = pltpu.get_barrier_semaphore()
    pl.semaphore_signal(barrier, inc=1, device_id=(row, other), device_id_type=MESH)

    def greet(n, carry):
        pl.semaphore_signal(
            barrier, inc=1, device_id=(lax.rem(row + n, 64), pan), device_id_type=MESH
        )
        return carry

    lax.fori_loop(1, 64, greet, 0, unroll=9)
    load_ranks.start()
    load_v[1].start()
    for n in range(1, 64):
        targets[n] = shifted(n, 1)

    load_g.wait()
    for q in range(2):
        state[0, q] = gin[q * CHUNK:(q + 1) * CHUNK, :].T

    components = lax.broadcasted_iota(jnp.int32, (8, width), 0) + 8 * pan

    def prepare_v(c, d):
        tiles = []
        for e in range(2):
            i = 2 * d + e
            rank = jnp.where(i == 2 * row + c, 0, ranks[c, i])
            tiles.append(jnp.where(components < rank, vf[c, i], 0.0))
        hi, lo = split(jnp.concatenate(tiles, axis=0))
        rows = pl.ds(pl.multiple_of(16 * d, 16), 16)
        vh[c, rows, :] = hi
        vl[c, rows, :] = lo

    def product(ah, al, operand):
        both = jnp.dot(ah[...], operand[...], preferred_element_type=F32)
        return (
            both[:, :CHUNK] + both[:, CHUNK:]
            + jnp.dot(al[...], operand[:, :CHUNK], preferred_element_type=F32)
        )

    def widen(target, value):
        hi, lo = split(value)
        target[:, :CHUNK] = hi
        target[:, CHUNK:] = lo

    def project(slot, c, value):
        operand = wide.at[pl.ds(0, width)]
        widen(operand, value)
        for start in range(0, 1024, MB):
            rows = pl.ds(start, MB)
            block = product(vh.at[c, rows], vl.at[c, rows], operand)
            send[slot, start // 16:(start + MB) // 16, c] = block.reshape(MB // 16, 2, 8, CHUNK)

    def message(slot, n, target):
        return pltpu.make_async_remote_copy(
            src_ref=send.at[slot, target],
            dst_ref=recv.at[slot, n],
            send_sem=send_sem.at[slot],
            recv_sem=recv_sem.at[slot, n // EARLY],
            device_id=(target, pan),
            device_id_type=MESH,
        )

    def all_messages(slot, late):
        cut = SHARED if slot == 3 else EARLY
        first, count = (cut, 64 - cut) if late else (1, cut - 1)
        return pltpu.make_async_remote_copy(
            src_ref=send.at[slot, pl.ds(first, count)],
            dst_ref=recv.at[slot, pl.ds(first, count)],
            send_sem=send_sem.at[slot],
            recv_sem=recv_sem.at[slot, late],
            device_id=(row, other),
            device_id_type=MESH,
        )

    def half_message(slot, n, target, c):
        return pltpu.make_async_remote_copy(
            src_ref=send.at[slot, target, c],
            dst_ref=recv.at[slot, n, c],
            send_sem=send_sem.at[slot],
            recv_sem=recv_sem.at[slot, n // EARLY],
            device_id=(target, pan),
            device_id_type=MESH,
        )

    def in_order(visit):
        for n in range(1, 4):
            visit(n)

        def body(m, carry):
            for n in range(4):
                visit(4 * m + n)
            return carry

        lax.fori_loop(1, 16, body, 0)

    def scatter(slot):
        in_order(lambda n: message(slot, n, targets[n]).start())
        recv[slot, 0] = send[slot, row]

    def last_message(n, target, kind):
        core = (pan, other)[kind]
        return pltpu.make_async_remote_copy(
            src_ref=send.at[3, target, :, core],
            dst_ref=recv_last.at[kind, n - SHARED],
            send_sem=send_sem.at[3],
            recv_sem=last_recv.at[kind],
            device_id=(target, core),
            device_id_type=MESH,
        )

    def all_last(kind):
        return pltpu.make_async_remote_copy(
            src_ref=recv_last.at[kind],
            dst_ref=recv_last.at[kind],
            send_sem=send_sem.at[3],
            recv_sem=last_recv.at[kind],
            device_id=(row, other),
            device_id_type=MESH,
        )

    def scatter_last():
        for n in range(1, 4):
            message(3, n, targets[n]).start()

        def early(m, carry):
            for n in range(4):
                message(3, 4 * m + n, targets[4 * m + n]).start()
            return carry

        lax.fori_loop(1, SHARED // 4, early, 0)

        def late(m, carry):
            for n in range(4):
                for kind in range(2):
                    last_message(4 * m + n, targets[4 * m + n], kind).start()
            return carry

        lax.fori_loop(SHARED // 4, 16, late, 0)
        recv[3, 0] = send[3, row]

    def scatter_half(slot, tile, beside=None):
        def visit(n):
            half_message(slot, n, targets[n], tile).start()
            if beside is not None:
                beside(n)

        if beside is not None:
            beside(0)
        in_order(visit)
        recv[slot, 0, tile] = send[slot, row, tile]

    def to_peer(source, target, sems, recvs, n):
        return pltpu.make_async_remote_copy(
            src_ref=source,
            dst_ref=target,
            send_sem=sems.at[n],
            recv_sem=recvs.at[n],
            device_id=(row, other),
            device_id_type=MESH,
        )

    def guess_copy(it, q):
        return to_peer(state.at[it, q], peer.at[it, q], g_send, g_recv, 2 * it + q)

    def low_copy(slot):
        return to_peer(low.at[slot], low_in.at[slot], l_send, l_recv, slot)

    load_v[0].wait()
    load_ranks.wait()

    def prepare_own(d, carry):
        prepare_v(pan, d)
        return carry

    lax.fori_loop(0, 64, prepare_own, 0, unroll=4)
    project(0, pan, state[0, 0])
    pl.semaphore_wait(barrier, 64)
    for q in range(2):
        guess_copy(0, q).start()
    load_v[1].wait()
    for load in (load_d, load_di, load_r, load_u):
        load.start()
    scatter_half(0, pan, lambda d: prepare_v(other, d))
    guess_copy(0, 0).wait_recv()
    project(0, other, peer[0, 0])
    scatter_half(0, other)
    project(1, pan, state[0, 1])
    guess_copy(0, 1).wait_recv()
    project(1, other, peer[0, 1])
    scatter(1)

    for n in range(64):
        sources[n] = shifted(n, -1)
    load_u.wait()

    def u_copy(m):
        return pltpu.make_async_remote_copy(
            src_ref=uf.at[other, pl.ds(2 * sources[SHARED + m], 2)],
            dst_ref=uf_peer.at[m],
            send_sem=u_send,
            recv_sem=u_recv,
            device_id=(row, other),
            device_id_type=MESH,
        )

    def start_u(m, carry):
        u_copy(m).start()
        return carry

    lax.fori_loop(0, LATE, start_u, 0)
    for i in range(2):
        def turn(m, carry):
            pieces = []
            for n in range(8):
                source = sources[8 * m + n]
                for e in range(2):
                    pieces.append(uf[i, 2 * source + e])
            hi, lo = split(jnp.concatenate(pieces, axis=0).T)
            columns = pl.ds(pl.multiple_of(128 * m, 128), 128)
            uth[i, :, columns] = hi
            utl[i, :, columns] = lo
            return carry

        lax.fori_loop(0, 8, turn, 0)
    all_u = pltpu.make_async_remote_copy(
        src_ref=uf_peer,
        dst_ref=uf_peer,
        send_sem=u_send,
        recv_sem=u_recv,
        device_id=(row, other),
        device_id_type=MESH,
    )
    all_u.wait_recv()
    for m in range(LATE // 8):
        hi, lo = split(uf_peer[8 * m:8 * m + 8].reshape(128, width).T)
        uth_peer[:, 128 * m:128 * m + 128] = hi
        utl_peer[:, 128 * m:128 * m + 128] = lo
    load_d.wait()
    dh[...], dl[...] = split(df[...])
    load_di.wait()
    dih[...], dil[...] = split(dif[...])
    load_r.wait()

    def subtract_dense(it, q):
        operand = wide.at[pl.ds(0, width)]
        widen(operand, state[it, q])
        dense[q] = rhs[q] - product(dh, dl, operand)

    for q in range(2):
        rhs[q] = rin[q * CHUNK:(q + 1) * CHUNK, :].T
        subtract_dense(0, q)

    def low_rank(slot, i, late):
        cut = SHARED if slot == 3 else EARLY
        first, count = (cut, 64 - cut) if late else (0, cut)
        columns = pl.ds(16 * first, 16 * count)
        operand = wide.at[columns]
        widen(operand, recv[slot, first:first + count, :, i].reshape(16 * count, CHUNK))
        return product(uth.at[i, :, columns], utl.at[i, :, columns], operand)

    def advance(it, q):
        slot = 2 * it + q
        all_messages(slot, 0).wait_recv()
        part[0] = low_rank(slot, other, 0)
        part[1] = low_rank(slot, pan, 0)
        all_messages(slot, 1).wait_recv()
        low[slot] = part[0] + low_rank(slot, other, 1)
        low_copy(slot).start()
        own = dense[q] - (part[1] + low_rank(slot, pan, 1))
        low_copy(slot).wait_recv()
        residual = own - low_in[slot]
        operand = wide.at[pl.ds(0, width)]
        widen(operand, residual)
        return residual, state[it, q] + product(dih, dil, operand)

    def advance_last():
        all_messages(3, 0).wait_recv()
        low[3] = low_rank(3, other, 0)
        low_copy(3).start()
        own = dense[1] - low_rank(3, pan, 0)
        low_copy(3).wait_recv()
        own = own - low_in[3]
        late = pl.ds(16 * SHARED, 16 * LATE)
        operand = wide.at[pl.ds(0, 16 * LATE)]
        all_last(0).wait_recv()
        widen(operand, recv_last[0].reshape(16 * LATE, CHUNK))
        own = own - product(uth.at[pan, :, late], utl.at[pan, :, late], operand)
        all_last(1).wait_recv()
        widen(operand, recv_last[1].reshape(16 * LATE, CHUNK))
        residual = own - product(uth_peer, utl_peer, operand)
        operand = wide.at[pl.ds(0, width)]
        widen(operand, residual)
        return residual, state[1, 1] + product(dih, dil, operand)

    for q in range(2):
        residual, guess = advance(0, q)
        state[1, q] = guess
        guess_copy(1, q).start()
        project(2 + q, pan, guess)
        guess_copy(1, q).wait_recv()
        project(2 + q, other, peer[1, q])
        if q == 0:
            scatter(2)
        else:
            scatter_last()
        subtract_dense(1, q)

    for q in range(2):
        residual, guess = advance(1, 0) if q == 0 else advance_last()
        result[0, q * CHUNK:(q + 1) * CHUNK] = guess.T
        result[1, q * CHUNK:(q + 1) * CHUNK] = residual.T

    all_u.wait_send()
    for slot in range(4):
        for late in range(2):
            all_messages(slot, late).wait_send()
        low_copy(slot).wait_send()
        guess_copy(slot // 2, slot % 2).wait_send()

def finish(result, sol_hbm, res_hbm, store_sem):
    stores = [
        pltpu.make_async_copy(result.at[n], target, store_sem.at[n])
        for n, target in enumerate((sol_hbm, res_hbm))
    ]
    for store in stores:
        store.start()
    for store in stores:
        store.wait()


def on_device(right_side, initial_guess, v_factor, u_factor, tile_ranks, diag_block, diag_inverse):
    any_space = pl.BlockSpec(memory_space=pl.ANY)
    tiles, count, part, width = v_factor.shape
    rhs_count = initial_guess.shape[0]
    shape = jax.ShapeDtypeStruct(initial_guess.shape, F32)
    result = pl.pallas_call(
        kernel,
        name="richardson",
        out_shape=pltpu.VMEM((2, rhs_count, width), F32),
        in_specs=[any_space] * 7,
        out_specs=pl.BlockSpec(memory_space=pltpu.VMEM),
        scratch_shapes=[
            pltpu.VMEM((rhs_count, width), F32),
            pltpu.VMEM((rhs_count, width), F32),
            pltpu.VMEM((tiles, count, part, width), F32),
            pltpu.VMEM((tiles, count * part, width), BF16),
            pltpu.VMEM((tiles, count * part, width), BF16),
            pltpu.VMEM((tiles, count, part, width), F32),
            pltpu.VMEM((tiles, width, count * part), BF16),
            pltpu.VMEM((tiles, width, count * part), BF16),
            pltpu.VMEM((width, width), F32),
            pltpu.VMEM((width, width), BF16),
            pltpu.VMEM((width, width), BF16),
            pltpu.VMEM((width, width), F32),
            pltpu.VMEM((width, width), BF16),
            pltpu.VMEM((width, width), BF16),
            pltpu.VMEM((2, width, CHUNK), F32),
            pltpu.VMEM((2, 2, width, CHUNK), F32),
            pltpu.VMEM((2, 2, width, CHUNK), F32),
            pltpu.VMEM((2, width, CHUNK), F32),
            pltpu.VMEM((4, width, CHUNK), F32),
            pltpu.VMEM((4, width, CHUNK), F32),
            pltpu.VMEM((2, width, CHUNK), F32),
            pltpu.VMEM((4, 64, tiles, tiles, part, CHUNK), F32),
            pltpu.VMEM((4, 64, tiles, tiles, part, CHUNK), F32),
            pltpu.VMEM((1024, 2 * CHUNK), BF16),
            pltpu.VMEM((LATE, tiles, part, width), F32),
            pltpu.VMEM((width, LATE * tiles * part), BF16),
            pltpu.VMEM((width, LATE * tiles * part), BF16),
            pltpu.VMEM((2, LATE, tiles, part, CHUNK), F32),
            pltpu.SMEM(tile_ranks.shape[::-1], jnp.int32),
            pltpu.SMEM((64,), jnp.int32),
            pltpu.SMEM((64,), jnp.int32),
            pltpu.SemaphoreType.DMA((8,)),
            pltpu.SemaphoreType.DMA((4,)),
            pltpu.SemaphoreType.DMA((4, 2)),
            pltpu.SemaphoreType.DMA((4,)),
            pltpu.SemaphoreType.DMA((4,)),
            pltpu.SemaphoreType.DMA((4,)),
            pltpu.SemaphoreType.DMA((4,)),
            pltpu.SemaphoreType.DMA,
            pltpu.SemaphoreType.DMA,
            pltpu.SemaphoreType.DMA((2,)),
        ],
        compiler_params=pltpu.CompilerParams(
            collective_id=0, has_side_effects=True, vmem_limit_bytes=58 << 20
        ),
    )(right_side, initial_guess, v_factor, u_factor, tile_ranks.T, diag_block, diag_inverse)
    return pl.pallas_call(
        finish,
        name="finish",
        out_shape=(shape, shape),
        in_specs=[pl.BlockSpec(memory_space=pltpu.VMEM)],
        out_specs=(any_space, any_space),
        scratch_shapes=[pltpu.SemaphoreType.DMA((2,))],
        compiler_params=pltpu.CompilerParams(vmem_limit_bytes=8 << 20),
    )(result)


def solution(mesh):
    placed = (
        P(None, "row"),
        P(None, ("row", "pan")),
        P("row", None, "pan", None),
        P("row", None, "pan", None),
        P(None, "row"),
        P(("row", "pan"), None),
        P(("row", "pan"), None),
    )
    return jax.shard_map(
        on_device,
        mesh=mesh,
        in_specs=placed,
        out_specs=(P(None, ("row", "pan")), P(None, ("row", "pan"))),
        check_vma=False,
    )
```

```python
import jax
import jax.numpy as jnp
from jax import lax
from jax.experimental import pallas as pl
from jax.experimental.pallas import tpu as pltpu
from jax.sharding import PartitionSpec as P

MESH = pl.DeviceIdType.MESH
F32 = jnp.float32
BF16 = jnp.bfloat16
CHUNK = 128
MB = 1024
EARLY = 40
SHARED = 32
LATE = 64 - SHARED


SHIFTS = [(-(a + b) % 4, (a + 2 * b + c) % 4, a) for c in range(4) for b in range(4) for a in range(4)]


def split(x):
    hi = x.astype(BF16)
    return hi, (x - hi.astype(F32)).astype(BF16)


def kernel(
    rhs_hbm, g_hbm, v_hbm, u_hbm, ranks_hbm, d_hbm, di_hbm, result,
    gin, rin, vf, vh, vl, uf, uth, utl, df, dh, dl, dif, dih, dil,
    rhs, state, peer, dense, low, low_in, part, send, recv, wide, uf_peer, uth_peer, utl_peer, recv_last,
    ranks, targets, sources, load_sem, send_sem, recv_sem, g_send, g_recv, l_send, l_recv, u_send, u_recv, last_recv,
):
    row = lax.axis_index("row")
    pan = lax.axis_index("pan")
    other = 1 - pan
    width = d_hbm.shape[0]
    z, y, x = row // 16, (row // 4) % 4, row % 4

    def shifted(n, sign):
        dz, dy, dx = SHIFTS[n]
        return (
            lax.rem(z + sign * dz + 4, 4) * 16
            + lax.rem(y + sign * dy + 4, 4) * 4
            + lax.rem(x + sign * dx + 4, 4)
        )

    load_g = pltpu.make_async_copy(g_hbm, gin, load_sem.at[0])
    load_v = [
        pltpu.make_async_copy(v_hbm.at[c], vf.at[c], load_sem.at[1 + n])
        for n, c in enumerate((pan, other))
    ]
    load_u = pltpu.make_async_copy(u_hbm, uf, load_sem.at[3])
    load_d = pltpu.make_async_copy(d_hbm, df, load_sem.at[4])
    load_di = pltpu.make_async_copy(di_hbm, dif, load_sem.at[5])
    own_columns = pl.ds(pl.multiple_of(pan * width, width), width)
    load_r = pltpu.make_async_copy(rhs_hbm.at[:, own_columns], rin, load_sem.at[6])
    load_ranks = pltpu.make_async_copy(ranks_hbm, ranks, load_sem.at[7])
    load_g.start()
    load_v[0].start()

    barrier = pltpu.get_barrier_semaphore()
    pl.semaphore_signal(barrier, inc=1, device_id=(row, other), device_id_type=MESH)

    def greet(n, carry):
        pl.semaphore_signal(
            barrier, inc=1, device_id=(lax.rem(row + n, 64), pan), device_id_type=MESH
        )
        return carry

    lax.fori_loop(1, 64, greet, 0, unroll=9)
    load_ranks.start()
    load_v[1].start()
    for n in range(1, 64):
        targets[n] = shifted(n, 1)

    load_g.wait()
    for q in range(2):
        state[0, q] = gin[q * CHUNK:(q + 1) * CHUNK, :].T

    components = lax.broadcasted_iota(jnp.int32, (8, width), 0) + 8 * pan

    def prepare_v(c, d):
        tiles = []
        for e in range(2):
            i = 2 * d + e
            rank = jnp.where(i == 2 * row + c, 0, ranks[c, i])
            tiles.append(jnp.where(components < rank, vf[c, i], 0.0))
        hi, lo = split(jnp.concatenate(tiles, axis=0))
        rows = pl.ds(pl.multiple_of(16 * d, 16), 16)
        vh[c, rows, :] = hi
        vl[c, rows, :] = lo

    def product(ah, al, operand):
        both = jnp.dot(ah[...], operand[...], preferred_element_type=F32)
        return (
            both[:, :CHUNK] + both[:, CHUNK:]
            + jnp.dot(al[...], operand[:, :CHUNK], preferred_element_type=F32)
        )

    def widen(target, value):
        hi, lo = split(value)
        target[:, :CHUNK] = hi
        target[:, CHUNK:] = lo

    def project(slot, c, value):
        operand = wide.at[pl.ds(0, width)]
        widen(operand, value)
        for start in range(0, 1024, MB):
            rows = pl.ds(start, MB)
            block = product(vh.at[c, rows], vl.at[c, rows], operand)
            send[slot, start // 16:(start + MB) // 16, c] = block.reshape(MB // 16, 2, 8, CHUNK)

    def message(slot, n, target):
        return pltpu.make_async_remote_copy(
            src_ref=send.at[slot, target],
            dst_ref=recv.at[slot, n],
            send_sem=send_sem.at[slot],
            recv_sem=recv_sem.at[slot, n // EARLY],
            device_id=(target, pan),
            device_id_type=MESH,
        )

    def all_messages(slot, late):
        cut = SHARED if slot == 3 else EARLY
        first, count = (cut, 64 - cut) if late else (1, cut - 1)
        return pltpu.make_async_remote_copy(
            src_ref=send.at[slot, pl.ds(first, count)],
            dst_ref=recv.at[slot, pl.ds(first, count)],
            send_sem=send_sem.at[slot],
            recv_sem=recv_sem.at[slot, late],
            device_id=(row, other),
            device_id_type=MESH,
        )

    def half_message(slot, n, target, c):
        return pltpu.make_async_remote_copy(
            src_ref=send.at[slot, target, c],
            dst_ref=recv.at[slot, n, c],
            send_sem=send_sem.at[slot],
            recv_sem=recv_sem.at[slot, n // EARLY],
            device_id=(target, pan),
            device_id_type=MESH,
        )

    def in_order(visit):
        def body(m, carry):
            for n in range(3):
                visit(1 + 3 * m + n)
            return carry

        lax.fori_loop(0, 21, body, 0)

    def scatter(slot):
        in_order(lambda n: message(slot, n, targets[n]).start())
        recv[slot, 0] = send[slot, row]

    def last_message(n, target, kind):
        core = (pan, other)[kind]
        return pltpu.make_async_remote_copy(
            src_ref=send.at[3, target, :, core],
            dst_ref=recv_last.at[kind, n - SHARED],
            send_sem=send_sem.at[3],
            recv_sem=last_recv.at[kind],
            device_id=(target, core),
            device_id_type=MESH,
        )

    def all_last(kind):
        return pltpu.make_async_remote_copy(
            src_ref=recv_last.at[kind],
            dst_ref=recv_last.at[kind],
            send_sem=send_sem.at[3],
            recv_sem=last_recv.at[kind],
            device_id=(row, other),
            device_id_type=MESH,
        )

    def scatter_last():
        for n in range(1, 4):
            message(3, n, targets[n]).start()

        def early(m, carry):
            for n in range(4):
                message(3, 4 * m + n, targets[4 * m + n]).start()
            return carry

        lax.fori_loop(1, SHARED // 4, early, 0)

        def late(m, carry):
            for n in range(4):
                for kind in range(2):
                    last_message(4 * m + n, targets[4 * m + n], kind).start()
            return carry

        lax.fori_loop(SHARED // 4, 16, late, 0)
        recv[3, 0] = send[3, row]

    def scatter_half(slot, tile, beside=None):
        def visit(n):
            half_message(slot, n, targets[n], tile).start()
            if beside is not None:
                beside(n)

        if beside is not None:
            beside(0)
        in_order(visit)
        recv[slot, 0, tile] = send[slot, row, tile]

    def to_peer(source, target, sems, recvs, n):
        return pltpu.make_async_remote_copy(
            src_ref=source,
            dst_ref=target,
            send_sem=sems.at[n],
            recv_sem=recvs.at[n],
            device_id=(row, other),
            device_id_type=MESH,
        )

    def guess_copy(it, q):
        return to_peer(state.at[it, q], peer.at[it, q], g_send, g_recv, 2 * it + q)

    def low_copy(slot):
        return to_peer(low.at[slot], low_in.at[slot], l_send, l_recv, slot)

    load_v[0].wait()
    load_ranks.wait()

    def prepare_own(d, carry):
        prepare_v(pan, d)
        return carry

    lax.fori_loop(0, 64, prepare_own, 0, unroll=4)
    project(0, pan, state[0, 0])
    pl.semaphore_wait(barrier, 64)
    for q in range(2):
        guess_copy(0, q).start()
    load_v[1].wait()
    for load in (load_d, load_di, load_r, load_u):
        load.start()
    scatter_half(0, pan, lambda d: prepare_v(other, d))
    guess_copy(0, 0).wait_recv()
    project(0, other, peer[0, 0])
    scatter_half(0, other)
    project(1, pan, state[0, 1])
    guess_copy(0, 1).wait_recv()
    project(1, other, peer[0, 1])
    scatter(1)

    for n in range(64):
        sources[n] = shifted(n, -1)
    load_u.wait()

    def u_copy(m):
        return pltpu.make_async_remote_copy(
            src_ref=uf.at[other, pl.ds(2 * sources[SHARED + m], 2)],
            dst_ref=uf_peer.at[m],
            send_sem=u_send,
            recv_sem=u_recv,
            device_id=(row, other),
            device_id_type=MESH,
        )

    def start_u(m, carry):
        u_copy(m).start()
        return carry

    lax.fori_loop(0, LATE, start_u, 0)
    for i in range(2):
        def turn(m, carry):
            pieces = []
            for n in range(8):
                source = sources[8 * m + n]
                for e in range(2):
                    pieces.append(uf[i, 2 * source + e])
            hi, lo = split(jnp.concatenate(pieces, axis=0).T)
            columns = pl.ds(pl.multiple_of(128 * m, 128), 128)
            uth[i, :, columns] = hi
            utl[i, :, columns] = lo
            return carry

        lax.fori_loop(0, 8, turn, 0)
    all_u = pltpu.make_async_remote_copy(
        src_ref=uf_peer,
        dst_ref=uf_peer,
        send_sem=u_send,
        recv_sem=u_recv,
        device_id=(row, other),
        device_id_type=MESH,
    )
    all_u.wait_recv()
    for m in range(LATE // 8):
        hi, lo = split(uf_peer[8 * m:8 * m + 8].reshape(128, width).T)
        uth_peer[:, 128 * m:128 * m + 128] = hi
        utl_peer[:, 128 * m:128 * m + 128] = lo
    load_d.wait()
    dh[...], dl[...] = split(df[...])
    load_di.wait()
    dih[...], dil[...] = split(dif[...])
    load_r.wait()

    def subtract_dense(it, q):
        operand = wide.at[pl.ds(0, width)]
        widen(operand, state[it, q])
        dense[q] = rhs[q] - product(dh, dl, operand)

    for q in range(2):
        rhs[q] = rin[q * CHUNK:(q + 1) * CHUNK, :].T
        subtract_dense(0, q)

    def low_rank(slot, i, late):
        cut = SHARED if slot == 3 else EARLY
        first, count = (cut, 64 - cut) if late else (0, cut)
        columns = pl.ds(16 * first, 16 * count)
        operand = wide.at[columns]
        widen(operand, recv[slot, first:first + count, :, i].reshape(16 * count, CHUNK))
        return product(uth.at[i, :, columns], utl.at[i, :, columns], operand)

    def advance(it, q):
        slot = 2 * it + q
        all_messages(slot, 0).wait_recv()
        part[0] = low_rank(slot, other, 0)
        part[1] = low_rank(slot, pan, 0)
        all_messages(slot, 1).wait_recv()
        low[slot] = part[0] + low_rank(slot, other, 1)
        low_copy(slot).start()
        own = dense[q] - (part[1] + low_rank(slot, pan, 1))
        low_copy(slot).wait_recv()
        residual = own - low_in[slot]
        operand = wide.at[pl.ds(0, width)]
        widen(operand, residual)
        return residual, state[it, q] + product(dih, dil, operand)

    def advance_last():
        all_messages(3, 0).wait_recv()
        low[3] = low_rank(3, other, 0)
        low_copy(3).start()
        own = dense[1] - low_rank(3, pan, 0)
        low_copy(3).wait_recv()
        own = own - low_in[3]
        late = pl.ds(16 * SHARED, 16 * LATE)
        operand = wide.at[pl.ds(0, 16 * LATE)]
        all_last(0).wait_recv()
        widen(operand, recv_last[0].reshape(16 * LATE, CHUNK))
        own = own - product(uth.at[pan, :, late], utl.at[pan, :, late], operand)
        all_last(1).wait_recv()
        widen(operand, recv_last[1].reshape(16 * LATE, CHUNK))
        residual = own - product(uth_peer, utl_peer, operand)
        operand = wide.at[pl.ds(0, width)]
        widen(operand, residual)
        return residual, state[1, 1] + product(dih, dil, operand)

    for q in range(2):
        residual, guess = advance(0, q)
        state[1, q] = guess
        guess_copy(1, q).start()
        project(2 + q, pan, guess)
        guess_copy(1, q).wait_recv()
        project(2 + q, other, peer[1, q])
        if q == 0:
            scatter(2)
        else:
            scatter_last()
        subtract_dense(1, q)

    for q in range(2):
        residual, guess = advance(1, 0) if q == 0 else advance_last()
        result[0, q * CHUNK:(q + 1) * CHUNK] = guess.T
        result[1, q * CHUNK:(q + 1) * CHUNK] = residual.T

    all_u.wait_send()
    for slot in range(4):
        for late in range(2):
            all_messages(slot, late).wait_send()
        low_copy(slot).wait_send()
        guess_copy(slot // 2, slot % 2).wait_send()

def finish(result, sol_hbm, res_hbm, store_sem):
    stores = [
        pltpu.make_async_copy(result.at[n], target, store_sem.at[n])
        for n, target in enumerate((sol_hbm, res_hbm))
    ]
    for store in stores:
        store.start()
    for store in stores:
        store.wait()


def on_device(right_side, initial_guess, v_factor, u_factor, tile_ranks, diag_block, diag_inverse):
    any_space = pl.BlockSpec(memory_space=pl.ANY)
    tiles, count, part, width = v_factor.shape
    rhs_count = initial_guess.shape[0]
    shape = jax.ShapeDtypeStruct(initial_guess.shape, F32)
    result = pl.pallas_call(
        kernel,
        name="richardson",
        out_shape=pltpu.VMEM((2, rhs_count, width), F32),
        in_specs=[any_space] * 7,
        out_specs=pl.BlockSpec(memory_space=pltpu.VMEM),
        scratch_shapes=[
            pltpu.VMEM((rhs_count, width), F32),
            pltpu.VMEM((rhs_count, width), F32),
            pltpu.VMEM((tiles, count, part, width), F32),
            pltpu.VMEM((tiles, count * part, width), BF16),
            pltpu.VMEM((tiles, count * part, width), BF16),
            pltpu.VMEM((tiles, count, part, width), F32),
            pltpu.VMEM((tiles, width, count * part), BF16),
            pltpu.VMEM((tiles, width, count * part), BF16),
            pltpu.VMEM((width, width), F32),
            pltpu.VMEM((width, width), BF16),
            pltpu.VMEM((width, width), BF16),
            pltpu.VMEM((width, width), F32),
            pltpu.VMEM((width, width), BF16),
            pltpu.VMEM((width, width), BF16),
            pltpu.VMEM((2, width, CHUNK), F32),
            pltpu.VMEM((2, 2, width, CHUNK), F32),
            pltpu.VMEM((2, 2, width, CHUNK), F32),
            pltpu.VMEM((2, width, CHUNK), F32),
            pltpu.VMEM((4, width, CHUNK), F32),
            pltpu.VMEM((4, width, CHUNK), F32),
            pltpu.VMEM((2, width, CHUNK), F32),
            pltpu.VMEM((4, 64, tiles, tiles, part, CHUNK), F32),
            pltpu.VMEM((4, 64, tiles, tiles, part, CHUNK), F32),
            pltpu.VMEM((1024, 2 * CHUNK), BF16),
            pltpu.VMEM((LATE, tiles, part, width), F32),
            pltpu.VMEM((width, LATE * tiles * part), BF16),
            pltpu.VMEM((width, LATE * tiles * part), BF16),
            pltpu.VMEM((2, LATE, tiles, part, CHUNK), F32),
            pltpu.SMEM(tile_ranks.shape[::-1], jnp.int32),
            pltpu.SMEM((64,), jnp.int32),
            pltpu.SMEM((64,), jnp.int32),
            pltpu.SemaphoreType.DMA((8,)),
            pltpu.SemaphoreType.DMA((4,)),
            pltpu.SemaphoreType.DMA((4, 2)),
            pltpu.SemaphoreType.DMA((4,)),
            pltpu.SemaphoreType.DMA((4,)),
            pltpu.SemaphoreType.DMA((4,)),
            pltpu.SemaphoreType.DMA((4,)),
            pltpu.SemaphoreType.DMA,
            pltpu.SemaphoreType.DMA,
            pltpu.SemaphoreType.DMA((2,)),
        ],
        compiler_params=pltpu.CompilerParams(
            collective_id=0, has_side_effects=True, vmem_limit_bytes=58 << 20
        ),
    )(right_side, initial_guess, v_factor, u_factor, tile_ranks.T, diag_block, diag_inverse)
    return pl.pallas_call(
        finish,
        name="finish",
        out_shape=(shape, shape),
        in_specs=[pl.BlockSpec(memory_space=pltpu.VMEM)],
        out_specs=(any_space, any_space),
        scratch_shapes=[pltpu.SemaphoreType.DMA((2,))],
        compiler_params=pltpu.CompilerParams(vmem_limit_bytes=8 << 20),
    )(result)


def solution(mesh):
    placed = (
        P(None, "row"),
        P(None, ("row", "pan")),
        P("row", None, "pan", None),
        P("row", None, "pan", None),
        P(None, "row"),
        P(("row", "pan"), None),
        P(("row", "pan"), None),
    )
    return jax.shard_map(
        on_device,
        mesh=mesh,
        in_specs=placed,
        out_specs=(P(None, ("row", "pan")), P(None, ("row", "pan"))),
        check_vma=False,
    )
```

```python
import jax
import jax.numpy as jnp
from jax import lax
from jax.experimental import pallas as pl
from jax.experimental.pallas import tpu as pltpu
from jax.sharding import PartitionSpec as P

MESH = pl.DeviceIdType.MESH
F32 = jnp.float32
BF16 = jnp.bfloat16
CHUNK = 128
MB = 1024
EARLY = 40
SHARED = 32
LATE = 64 - SHARED


SHIFTS = [(-(a + b) % 4, (a + 2 * b + c) % 4, a) for c in range(4) for b in range(4) for a in range(4)]


def split(x):
    hi = x.astype(BF16)
    return hi, (x - hi.astype(F32)).astype(BF16)


def kernel(
    rhs_hbm, g_hbm, v_hbm, u_hbm, ranks_hbm, d_hbm, di_hbm, result,
    gin, rin, vf, vh, vl, uf, uth, utl, df, dh, dl, dif, dih, dil,
    rhs, state, peer, dense, low, low_in, part, send, recv, wide, uf_peer, uth_peer, utl_peer, recv_last,
    ranks, targets, sources, load_sem, send_sem, recv_sem, g_send, g_recv, l_send, l_recv, u_send, u_recv, last_recv,
):
    row = lax.axis_index("row")
    pan = lax.axis_index("pan")
    other = 1 - pan
    width = d_hbm.shape[0]
    z, y, x = row // 16, (row // 4) % 4, row % 4

    def shifted(n, sign):
        dz, dy, dx = SHIFTS[n]
        return (
            lax.rem(z + sign * dz + 4, 4) * 16
            + lax.rem(y + sign * dy + 4, 4) * 4
            + lax.rem(x + sign * dx + 4, 4)
        )

    load_g = pltpu.make_async_copy(g_hbm, gin, load_sem.at[0])
    load_v = [
        pltpu.make_async_copy(v_hbm.at[c], vf.at[c], load_sem.at[1 + n])
        for n, c in enumerate((pan, other))
    ]
    load_u = pltpu.make_async_copy(u_hbm, uf, load_sem.at[3])
    load_d = pltpu.make_async_copy(d_hbm, df, load_sem.at[4])
    load_di = pltpu.make_async_copy(di_hbm, dif, load_sem.at[5])
    own_columns = pl.ds(pl.multiple_of(pan * width, width), width)
    load_r = pltpu.make_async_copy(rhs_hbm.at[:, own_columns], rin, load_sem.at[6])
    load_ranks = pltpu.make_async_copy(ranks_hbm, ranks, load_sem.at[7])

    barrier = pltpu.get_barrier_semaphore()
    pl.semaphore_signal(barrier, inc=1, device_id=(row, other), device_id_type=MESH)

    def greet(n, carry):
        pl.semaphore_signal(
            barrier, inc=1, device_id=(lax.rem(row + n, 64), pan), device_id_type=MESH
        )
        return carry

    lax.fori_loop(1, 64, greet, 0, unroll=9)
    load_g.start()
    load_v[0].start()
    load_ranks.start()
    load_v[1].start()
    for n in range(1, 64):
        targets[n] = shifted(n, 1)

    load_g.wait()
    state[0, 0] = gin[:CHUNK, :].T

    components = lax.broadcasted_iota(jnp.int32, (8, width), 0) + 8 * pan

    def prepare_v(c, d):
        tiles = []
        for e in range(2):
            i = 2 * d + e
            rank = jnp.where(i == 2 * row + c, 0, ranks[c, i])
            tiles.append(jnp.where(components < rank, vf[c, i], 0.0))
        hi, lo = split(jnp.concatenate(tiles, axis=0))
        rows = pl.ds(pl.multiple_of(16 * d, 16), 16)
        vh[c, rows, :] = hi
        vl[c, rows, :] = lo

    def product(ah, al, operand):
        both = jnp.dot(ah[...], operand[...], preferred_element_type=F32)
        return (
            both[:, :CHUNK] + both[:, CHUNK:]
            + jnp.dot(al[...], operand[:, :CHUNK], preferred_element_type=F32)
        )

    def widen(target, value):
        hi, lo = split(value)
        target[:, :CHUNK] = hi
        target[:, CHUNK:] = lo

    def project(slot, c, value):
        operand = wide.at[pl.ds(0, width)]
        widen(operand, value)
        for start in range(0, 1024, MB):
            rows = pl.ds(start, MB)
            block = product(vh.at[c, rows], vl.at[c, rows], operand)
            send[slot, start // 16:(start + MB) // 16, c] = block.reshape(MB // 16, 2, 8, CHUNK)

    def message(slot, n, target):
        return pltpu.make_async_remote_copy(
            src_ref=send.at[slot, target],
            dst_ref=recv.at[slot, n],
            send_sem=send_sem.at[slot],
            recv_sem=recv_sem.at[slot, n // EARLY],
            device_id=(target, pan),
            device_id_type=MESH,
        )

    def all_messages(slot, late):
        cut = SHARED if slot == 3 else EARLY
        first, count = (cut, 64 - cut) if late else (1, cut - 1)
        return pltpu.make_async_remote_copy(
            src_ref=send.at[slot, pl.ds(first, count)],
            dst_ref=recv.at[slot, pl.ds(first, count)],
            send_sem=send_sem.at[slot],
            recv_sem=recv_sem.at[slot, late],
            device_id=(row, other),
            device_id_type=MESH,
        )

    def half_message(slot, n, target, c):
        return pltpu.make_async_remote_copy(
            src_ref=send.at[slot, target, c],
            dst_ref=recv.at[slot, n, c],
            send_sem=send_sem.at[slot],
            recv_sem=recv_sem.at[slot, n // EARLY],
            device_id=(target, pan),
            device_id_type=MESH,
        )

    def in_order(visit):
        def body(m, carry):
            for n in range(3):
                visit(1 + 3 * m + n)
            return carry

        lax.fori_loop(0, 21, body, 0)

    def scatter(slot):
        in_order(lambda n: message(slot, n, targets[n]).start())
        recv[slot, 0] = send[slot, row]

    def last_message(n, target, kind):
        core = (pan, other)[kind]
        return pltpu.make_async_remote_copy(
            src_ref=send.at[3, target, :, core],
            dst_ref=recv_last.at[kind, n - SHARED],
            send_sem=send_sem.at[3],
            recv_sem=last_recv.at[kind],
            device_id=(target, core),
            device_id_type=MESH,
        )

    def all_last(kind):
        return pltpu.make_async_remote_copy(
            src_ref=recv_last.at[kind],
            dst_ref=recv_last.at[kind],
            send_sem=send_sem.at[3],
            recv_sem=last_recv.at[kind],
            device_id=(row, other),
            device_id_type=MESH,
        )

    def scatter_last():
        for n in range(1, 4):
            message(3, n, targets[n]).start()

        def early(m, carry):
            for n in range(4):
                message(3, 4 * m + n, targets[4 * m + n]).start()
            return carry

        lax.fori_loop(1, SHARED // 4, early, 0)

        def late(m, carry):
            for n in range(4):
                for kind in range(2):
                    last_message(4 * m + n, targets[4 * m + n], kind).start()
            return carry

        lax.fori_loop(SHARED // 4, 16, late, 0)
        recv[3, 0] = send[3, row]

    def scatter_half(slot, tile, beside=None):
        def visit(n):
            half_message(slot, n, targets[n], tile).start()
            if beside is not None:
                beside(n)

        if beside is not None:
            beside(0)
        in_order(visit)
        recv[slot, 0, tile] = send[slot, row, tile]

    def to_peer(source, target, sems, recvs, n):
        return pltpu.make_async_remote_copy(
            src_ref=source,
            dst_ref=target,
            send_sem=sems.at[n],
            recv_sem=recvs.at[n],
            device_id=(row, other),
            device_id_type=MESH,
        )

    def guess_copy(it, q):
        return to_peer(state.at[it, q], peer.at[it, q], g_send, g_recv, 2 * it + q)

    def low_copy(slot):
        return to_peer(low.at[slot], low_in.at[slot], l_send, l_recv, slot)

    load_v[0].wait()
    load_ranks.wait()

    def prepare_own(d, carry):
        prepare_v(pan, d)
        return carry

    lax.fori_loop(0, 64, prepare_own, 0, unroll=4)
    project(0, pan, state[0, 0])
    pl.semaphore_wait(barrier, 64)
    guess_copy(0, 0).start()
    load_v[1].wait()
    for load in (load_d, load_di, load_r, load_u):
        load.start()
    scatter_half(0, pan, lambda d: prepare_v(other, d))
    state[0, 1] = gin[CHUNK:, :].T
    guess_copy(0, 1).start()
    guess_copy(0, 0).wait_recv()
    project(0, other, peer[0, 0])
    scatter_half(0, other)
    project(1, pan, state[0, 1])
    guess_copy(0, 1).wait_recv()
    project(1, other, peer[0, 1])
    scatter(1)

    for n in range(64):
        sources[n] = shifted(n, -1)
    load_u.wait()

    def u_copy(m):
        return pltpu.make_async_remote_copy(
            src_ref=uf.at[other, pl.ds(2 * sources[SHARED + m], 2)],
            dst_ref=uf_peer.at[m],
            send_sem=u_send,
            recv_sem=u_recv,
            device_id=(row, other),
            device_id_type=MESH,
        )

    def start_u(m, carry):
        u_copy(m).start()
        return carry

    lax.fori_loop(0, LATE, start_u, 0)
    for i in range(2):
        def turn(m, carry):
            pieces = []
            for n in range(8):
                source = sources[8 * m + n]
                for e in range(2):
                    pieces.append(uf[i, 2 * source + e])
            hi, lo = split(jnp.concatenate(pieces, axis=0).T)
            columns = pl.ds(pl.multiple_of(128 * m, 128), 128)
            uth[i, :, columns] = hi
            utl[i, :, columns] = lo
            return carry

        lax.fori_loop(0, 8, turn, 0)
    all_u = pltpu.make_async_remote_copy(
        src_ref=uf_peer,
        dst_ref=uf_peer,
        send_sem=u_send,
        recv_sem=u_recv,
        device_id=(row, other),
        device_id_type=MESH,
    )
    all_u.wait_recv()
    for m in range(LATE // 8):
        hi, lo = split(uf_peer[8 * m:8 * m + 8].reshape(128, width).T)
        uth_peer[:, 128 * m:128 * m + 128] = hi
        utl_peer[:, 128 * m:128 * m + 128] = lo
    load_d.wait()
    dh[...], dl[...] = split(df[...])
    load_di.wait()
    dih[...], dil[...] = split(dif[...])
    load_r.wait()

    def subtract_dense(it, q):
        operand = wide.at[pl.ds(0, width)]
        widen(operand, state[it, q])
        dense[q] = rhs[q] - product(dh, dl, operand)

    for q in range(2):
        rhs[q] = rin[q * CHUNK:(q + 1) * CHUNK, :].T
        subtract_dense(0, q)

    def low_rank(slot, i, late):
        cut = SHARED if slot == 3 else EARLY
        first, count = (cut, 64 - cut) if late else (0, cut)
        columns = pl.ds(16 * first, 16 * count)
        operand = wide.at[columns]
        widen(operand, recv[slot, first:first + count, :, i].reshape(16 * count, CHUNK))
        return product(uth.at[i, :, columns], utl.at[i, :, columns], operand)

    def advance(it, q):
        slot = 2 * it + q
        all_messages(slot, 0).wait_recv()
        part[0] = low_rank(slot, other, 0)
        part[1] = low_rank(slot, pan, 0)
        all_messages(slot, 1).wait_recv()
        low[slot] = part[0] + low_rank(slot, other, 1)
        low_copy(slot).start()
        own = dense[q] - (part[1] + low_rank(slot, pan, 1))
        low_copy(slot).wait_recv()
        residual = own - low_in[slot]
        operand = wide.at[pl.ds(0, width)]
        widen(operand, residual)
        return residual, state[it, q] + product(dih, dil, operand)

    def advance_last():
        all_messages(3, 0).wait_recv()
        low[3] = low_rank(3, other, 0)
        low_copy(3).start()
        own = dense[1] - low_rank(3, pan, 0)
        low_copy(3).wait_recv()
        own = own - low_in[3]
        late = pl.ds(16 * SHARED, 16 * LATE)
        operand = wide.at[pl.ds(0, 16 * LATE)]
        all_last(0).wait_recv()
        widen(operand, recv_last[0].reshape(16 * LATE, CHUNK))
        own = own - product(uth.at[pan, :, late], utl.at[pan, :, late], operand)
        all_last(1).wait_recv()
        widen(operand, recv_last[1].reshape(16 * LATE, CHUNK))
        residual = own - product(uth_peer, utl_peer, operand)
        operand = wide.at[pl.ds(0, width)]
        widen(operand, residual)
        return residual, state[1, 1] + product(dih, dil, operand)

    for q in range(2):
        residual, guess = advance(0, q)
        state[1, q] = guess
        guess_copy(1, q).start()
        project(2 + q, pan, guess)
        guess_copy(1, q).wait_recv()
        project(2 + q, other, peer[1, q])
        if q == 0:
            scatter(2)
        else:
            scatter_last()
        subtract_dense(1, q)

    for q in range(2):
        residual, guess = advance(1, 0) if q == 0 else advance_last()
        result[0, q * CHUNK:(q + 1) * CHUNK] = guess.T
        result[1, q * CHUNK:(q + 1) * CHUNK] = residual.T

    all_u.wait_send()
    for slot in range(4):
        for late in range(2):
            all_messages(slot, late).wait_send()
        low_copy(slot).wait_send()
        guess_copy(slot // 2, slot % 2).wait_send()

def finish(result, sol_hbm, res_hbm, store_sem):
    stores = [
        pltpu.make_async_copy(result.at[n], target, store_sem.at[n])
        for n, target in enumerate((sol_hbm, res_hbm))
    ]
    for store in stores:
        store.start()
    for store in stores:
        store.wait()


def on_device(right_side, initial_guess, v_factor, u_factor, tile_ranks, diag_block, diag_inverse):
    any_space = pl.BlockSpec(memory_space=pl.ANY)
    tiles, count, part, width = v_factor.shape
    rhs_count = initial_guess.shape[0]
    shape = jax.ShapeDtypeStruct(initial_guess.shape, F32)
    result = pl.pallas_call(
        kernel,
        name="richardson",
        out_shape=pltpu.VMEM((2, rhs_count, width), F32),
        in_specs=[any_space] * 7,
        out_specs=pl.BlockSpec(memory_space=pltpu.VMEM),
        scratch_shapes=[
            pltpu.VMEM((rhs_count, width), F32),
            pltpu.VMEM((rhs_count, width), F32),
            pltpu.VMEM((tiles, count, part, width), F32),
            pltpu.VMEM((tiles, count * part, width), BF16),
            pltpu.VMEM((tiles, count * part, width), BF16),
            pltpu.VMEM((tiles, count, part, width), F32),
            pltpu.VMEM((tiles, width, count * part), BF16),
            pltpu.VMEM((tiles, width, count * part), BF16),
            pltpu.VMEM((width, width), F32),
            pltpu.VMEM((width, width), BF16),
            pltpu.VMEM((width, width), BF16),
            pltpu.VMEM((width, width), F32),
            pltpu.VMEM((width, width), BF16),
            pltpu.VMEM((width, width), BF16),
            pltpu.VMEM((2, width, CHUNK), F32),
            pltpu.VMEM((2, 2, width, CHUNK), F32),
            pltpu.VMEM((2, 2, width, CHUNK), F32),
            pltpu.VMEM((2, width, CHUNK), F32),
            pltpu.VMEM((4, width, CHUNK), F32),
            pltpu.VMEM((4, width, CHUNK), F32),
            pltpu.VMEM((2, width, CHUNK), F32),
            pltpu.VMEM((4, 64, tiles, tiles, part, CHUNK), F32),
            pltpu.VMEM((4, 64, tiles, tiles, part, CHUNK), F32),
            pltpu.VMEM((1024, 2 * CHUNK), BF16),
            pltpu.VMEM((LATE, tiles, part, width), F32),
            pltpu.VMEM((width, LATE * tiles * part), BF16),
            pltpu.VMEM((width, LATE * tiles * part), BF16),
            pltpu.VMEM((2, LATE, tiles, part, CHUNK), F32),
            pltpu.SMEM(tile_ranks.shape[::-1], jnp.int32),
            pltpu.SMEM((64,), jnp.int32),
            pltpu.SMEM((64,), jnp.int32),
            pltpu.SemaphoreType.DMA((8,)),
            pltpu.SemaphoreType.DMA((4,)),
            pltpu.SemaphoreType.DMA((4, 2)),
            pltpu.SemaphoreType.DMA((4,)),
            pltpu.SemaphoreType.DMA((4,)),
            pltpu.SemaphoreType.DMA((4,)),
            pltpu.SemaphoreType.DMA((4,)),
            pltpu.SemaphoreType.DMA,
            pltpu.SemaphoreType.DMA,
            pltpu.SemaphoreType.DMA((2,)),
        ],
        compiler_params=pltpu.CompilerParams(
            collective_id=0, has_side_effects=True, vmem_limit_bytes=58 << 20
        ),
    )(right_side, initial_guess, v_factor, u_factor, tile_ranks.T, diag_block, diag_inverse)
    return pl.pallas_call(
        finish,
        name="finish",
        out_shape=(shape, shape),
        in_specs=[pl.BlockSpec(memory_space=pltpu.VMEM)],
        out_specs=(any_space, any_space),
        scratch_shapes=[pltpu.SemaphoreType.DMA((2,))],
        compiler_params=pltpu.CompilerParams(vmem_limit_bytes=8 << 20),
    )(result)


def solution(mesh):
    placed = (
        P(None, "row"),
        P(None, ("row", "pan")),
        P("row", None, "pan", None),
        P("row", None, "pan", None),
        P(None, "row"),
        P(("row", "pan"), None),
        P(("row", "pan"), None),
    )
    return jax.shard_map(
        on_device,
        mesh=mesh,
        in_specs=placed,
        out_specs=(P(None, ("row", "pan")), P(None, ("row", "pan"))),
        check_vma=False,
    )
```

```python
import jax
import jax.numpy as jnp
from jax import lax
from jax.experimental import pallas as pl
from jax.experimental.pallas import tpu as pltpu
from jax.sharding import PartitionSpec as P

MESH = pl.DeviceIdType.MESH
F32 = jnp.float32
BF16 = jnp.bfloat16
CHUNK = 128
MB = 1024
EARLY = 48
SHARED = 32
LATE = 64 - SHARED


SHIFTS = [(-(a + b) % 4, (a + 2 * b + c) % 4, a) for c in range(4) for b in range(4) for a in range(4)]


def split(x):
    hi = x.astype(BF16)
    return hi, (x - hi.astype(F32)).astype(BF16)


def kernel(
    rhs_hbm, g_hbm, v_hbm, u_hbm, ranks_hbm, d_hbm, di_hbm, result,
    gin, rin, vf, vh, vl, uf, uth, utl, df, dh, dl, dif, dih, dil,
    rhs, state, peer, dense, low, low_in, part, send, recv, wide, uf_peer, uth_peer, utl_peer, recv_last,
    ranks, targets, sources, load_sem, send_sem, recv_sem, g_send, g_recv, l_send, l_recv, u_send, u_recv, last_recv,
):
    row = lax.axis_index("row")
    pan = lax.axis_index("pan")
    other = 1 - pan
    width = d_hbm.shape[0]
    z, y, x = row // 16, (row // 4) % 4, row % 4

    def shifted(n, sign):
        dz, dy, dx = SHIFTS[n]
        return (
            lax.rem(z + sign * dz + 4, 4) * 16
            + lax.rem(y + sign * dy + 4, 4) * 4
            + lax.rem(x + sign * dx + 4, 4)
        )

    load_g = pltpu.make_async_copy(g_hbm, gin, load_sem.at[0])
    load_v = [
        pltpu.make_async_copy(v_hbm.at[c], vf.at[c], load_sem.at[1 + n])
        for n, c in enumerate((pan, other))
    ]
    load_u = pltpu.make_async_copy(u_hbm, uf, load_sem.at[3])
    load_d = pltpu.make_async_copy(d_hbm, df, load_sem.at[4])
    load_di = pltpu.make_async_copy(di_hbm, dif, load_sem.at[5])
    own_columns = pl.ds(pl.multiple_of(pan * width, width), width)
    load_r = pltpu.make_async_copy(rhs_hbm.at[:, own_columns], rin, load_sem.at[6])
    load_ranks = pltpu.make_async_copy(ranks_hbm, ranks, load_sem.at[7])
    load_g.start()
    load_v[0].start()

    barrier = pltpu.get_barrier_semaphore()
    pl.semaphore_signal(barrier, inc=1, device_id=(row, other), device_id_type=MESH)

    def greet(n, carry):
        pl.semaphore_signal(
            barrier, inc=1, device_id=(lax.rem(row + n, 64), pan), device_id_type=MESH
        )
        return carry

    lax.fori_loop(1, 64, greet, 0, unroll=9)
    load_ranks.start()
    load_v[1].start()
    for n in range(1, 64):
        targets[n] = shifted(n, 1)

    load_g.wait()
    for q in range(2):
        state[0, q] = gin[q * CHUNK:(q + 1) * CHUNK, :].T

    components = lax.broadcasted_iota(jnp.int32, (8, width), 0) + 8 * pan

    def prepare_v(c, d):
        tiles = []
        for e in range(2):
            i = 2 * d + e
            rank = jnp.where(i == 2 * row + c, 0, ranks[c, i])
            tiles.append(jnp.where(components < rank, vf[c, i], 0.0))
        hi, lo = split(jnp.concatenate(tiles, axis=0))
        rows = pl.ds(pl.multiple_of(16 * d, 16), 16)
        vh[c, rows, :] = hi
        vl[c, rows, :] = lo

    def product(ah, al, operand):
        both = jnp.dot(ah[...], operand[...], preferred_element_type=F32)
        return (
            both[:, :CHUNK] + both[:, CHUNK:]
            + jnp.dot(al[...], operand[:, :CHUNK], preferred_element_type=F32)
        )

    def widen(target, value):
        hi, lo = split(value)
        target[:, :CHUNK] = hi
        target[:, CHUNK:] = lo

    def project(slot, c, value):
        operand = wide.at[pl.ds(0, width)]
        widen(operand, value)
        for start in range(0, 1024, MB):
            rows = pl.ds(start, MB)
            block = product(vh.at[c, rows], vl.at[c, rows], operand)
            send[slot, start // 16:(start + MB) // 16, c] = block.reshape(MB // 16, 2, 8, CHUNK)

    def message(slot, n, target):
        return pltpu.make_async_remote_copy(
            src_ref=send.at[slot, target],
            dst_ref=recv.at[slot, n],
            send_sem=send_sem.at[slot],
            recv_sem=recv_sem.at[slot, n // EARLY],
            device_id=(target, pan),
            device_id_type=MESH,
        )

    def all_messages(slot, late):
        cut = SHARED if slot == 3 else EARLY
        first, count = (cut, 64 - cut) if late else (1, cut - 1)
        return pltpu.make_async_remote_copy(
            src_ref=send.at[slot, pl.ds(first, count)],
            dst_ref=recv.at[slot, pl.ds(first, count)],
            send_sem=send_sem.at[slot],
            recv_sem=recv_sem.at[slot, late],
            device_id=(row, other),
            device_id_type=MESH,
        )

    def half_message(slot, n, target, c):
        return pltpu.make_async_remote_copy(
            src_ref=send.at[slot, target, c],
            dst_ref=recv.at[slot, n, c],
            send_sem=send_sem.at[slot],
            recv_sem=recv_sem.at[slot, n // EARLY],
            device_id=(target, pan),
            device_id_type=MESH,
        )

    def in_order(visit):
        def body(m, carry):
            for n in range(3):
                visit(1 + 3 * m + n)
            return carry

        lax.fori_loop(0, 21, body, 0)

    def scatter(slot):
        in_order(lambda n: message(slot, n, targets[n]).start())
        recv[slot, 0] = send[slot, row]

    def last_message(n, target, kind):
        core = (pan, other)[kind]
        return pltpu.make_async_remote_copy(
            src_ref=send.at[3, target, :, core],
            dst_ref=recv_last.at[kind, n - SHARED],
            send_sem=send_sem.at[3],
            recv_sem=last_recv.at[kind],
            device_id=(target, core),
            device_id_type=MESH,
        )

    def all_last(kind):
        return pltpu.make_async_remote_copy(
            src_ref=recv_last.at[kind],
            dst_ref=recv_last.at[kind],
            send_sem=send_sem.at[3],
            recv_sem=last_recv.at[kind],
            device_id=(row, other),
            device_id_type=MESH,
        )

    def scatter_last():
        for n in range(1, 4):
            message(3, n, targets[n]).start()

        def early(m, carry):
            for n in range(4):
                message(3, 4 * m + n, targets[4 * m + n]).start()
            return carry

        lax.fori_loop(1, SHARED // 4, early, 0)

        def late(m, carry):
            for n in range(4):
                for kind in range(2):
                    last_message(4 * m + n, targets[4 * m + n], kind).start()
            return carry

        lax.fori_loop(SHARED // 4, 16, late, 0)
        recv[3, 0] = send[3, row]

    def scatter_half(slot, tile, beside=None):
        def visit(n):
            half_message(slot, n, targets[n], tile).start()
            if beside is not None:
                beside(n)

        if beside is not None:
            beside(0)
        in_order(visit)
        recv[slot, 0, tile] = send[slot, row, tile]

    def to_peer(source, target, sems, recvs, n):
        return pltpu.make_async_remote_copy(
            src_ref=source,
            dst_ref=target,
            send_sem=sems.at[n],
            recv_sem=recvs.at[n],
            device_id=(row, other),
            device_id_type=MESH,
        )

    def guess_copy(it, q):
        return to_peer(state.at[it, q], peer.at[it, q], g_send, g_recv, 2 * it + q)

    def low_copy(slot):
        return to_peer(low.at[slot], low_in.at[slot], l_send, l_recv, slot)

    load_v[0].wait()
    load_ranks.wait()

    def prepare_own(d, carry):
        prepare_v(pan, d)
        return carry

    lax.fori_loop(0, 64, prepare_own, 0, unroll=4)
    project(0, pan, state[0, 0])
    pl.semaphore_wait(barrier, 64)
    for q in range(2):
        guess_copy(0, q).start()
    load_v[1].wait()
    for load in (load_d, load_di, load_r, load_u):
        load.start()
    scatter_half(0, pan, lambda d: prepare_v(other, d))
    guess_copy(0, 0).wait_recv()
    project(0, other, peer[0, 0])
    scatter_half(0, other)
    project(1, pan, state[0, 1])
    guess_copy(0, 1).wait_recv()
    project(1, other, peer[0, 1])
    scatter(1)

    for n in range(64):
        sources[n] = shifted(n, -1)
    load_u.wait()

    def u_copy(m):
        return pltpu.make_async_remote_copy(
            src_ref=uf.at[other, pl.ds(2 * sources[SHARED + m], 2)],
            dst_ref=uf_peer.at[m],
            send_sem=u_send,
            recv_sem=u_recv,
            device_id=(row, other),
            device_id_type=MESH,
        )

    def start_u(m, carry):
        u_copy(m).start()
        return carry

    lax.fori_loop(0, LATE, start_u, 0)
    for i in range(2):
        def turn(m, carry):
            pieces = []
            for n in range(8):
                source = sources[8 * m + n]
                for e in range(2):
                    pieces.append(uf[i, 2 * source + e])
            hi, lo = split(jnp.concatenate(pieces, axis=0).T)
            columns = pl.ds(pl.multiple_of(128 * m, 128), 128)
            uth[i, :, columns] = hi
            utl[i, :, columns] = lo
            return carry

        lax.fori_loop(0, 8, turn, 0)
    all_u = pltpu.make_async_remote_copy(
        src_ref=uf_peer,
        dst_ref=uf_peer,
        send_sem=u_send,
        recv_sem=u_recv,
        device_id=(row, other),
        device_id_type=MESH,
    )
    all_u.wait_recv()
    for m in range(LATE // 8):
        hi, lo = split(uf_peer[8 * m:8 * m + 8].reshape(128, width).T)
        uth_peer[:, 128 * m:128 * m + 128] = hi
        utl_peer[:, 128 * m:128 * m + 128] = lo
    load_d.wait()
    dh[...], dl[...] = split(df[...])
    load_di.wait()
    dih[...], dil[...] = split(dif[...])
    load_r.wait()

    def subtract_dense(it, q):
        operand = wide.at[pl.ds(0, width)]
        widen(operand, state[it, q])
        dense[q] = rhs[q] - product(dh, dl, operand)

    for q in range(2):
        rhs[q] = rin[q * CHUNK:(q + 1) * CHUNK, :].T
        subtract_dense(0, q)

    def low_rank(slot, i, late):
        cut = SHARED if slot == 3 else EARLY
        first, count = (cut, 64 - cut) if late else (0, cut)
        columns = pl.ds(16 * first, 16 * count)
        operand = wide.at[columns]
        widen(operand, recv[slot, first:first + count, :, i].reshape(16 * count, CHUNK))
        return product(uth.at[i, :, columns], utl.at[i, :, columns], operand)

    def advance(it, q):
        slot = 2 * it + q
        all_messages(slot, 0).wait_recv()
        part[0] = low_rank(slot, other, 0)
        part[1] = low_rank(slot, pan, 0)
        all_messages(slot, 1).wait_recv()
        low[slot] = part[0] + low_rank(slot, other, 1)
        low_copy(slot).start()
        own = dense[q] - (part[1] + low_rank(slot, pan, 1))
        low_copy(slot).wait_recv()
        residual = own - low_in[slot]
        operand = wide.at[pl.ds(0, width)]
        widen(operand, residual)
        return residual, state[it, q] + product(dih, dil, operand)

    def advance_last():
        all_messages(3, 0).wait_recv()
        low[3] = low_rank(3, other, 0)
        low_copy(3).start()
        own = dense[1] - low_rank(3, pan, 0)
        low_copy(3).wait_recv()
        own = own - low_in[3]
        late = pl.ds(16 * SHARED, 16 * LATE)
        operand = wide.at[pl.ds(0, 16 * LATE)]
        all_last(0).wait_recv()
        widen(operand, recv_last[0].reshape(16 * LATE, CHUNK))
        own = own - product(uth.at[pan, :, late], utl.at[pan, :, late], operand)
        all_last(1).wait_recv()
        widen(operand, recv_last[1].reshape(16 * LATE, CHUNK))
        residual = own - product(uth_peer, utl_peer, operand)
        operand = wide.at[pl.ds(0, width)]
        widen(operand, residual)
        return residual, state[1, 1] + product(dih, dil, operand)

    for q in range(2):
        residual, guess = advance(0, q)
        state[1, q] = guess
        guess_copy(1, q).start()
        project(2 + q, pan, guess)
        guess_copy(1, q).wait_recv()
        project(2 + q, other, peer[1, q])
        if q == 0:
            scatter(2)
        else:
            scatter_last()
        subtract_dense(1, q)

    for q in range(2):
        residual, guess = advance(1, 0) if q == 0 else advance_last()
        result[0, q * CHUNK:(q + 1) * CHUNK] = guess.T
        result[1, q * CHUNK:(q + 1) * CHUNK] = residual.T

    all_u.wait_send()
    for slot in range(4):
        for late in range(2):
            all_messages(slot, late).wait_send()
        low_copy(slot).wait_send()
        guess_copy(slot // 2, slot % 2).wait_send()

def finish(result, sol_hbm, res_hbm, store_sem):
    stores = [
        pltpu.make_async_copy(result.at[n], target, store_sem.at[n])
        for n, target in enumerate((sol_hbm, res_hbm))
    ]
    for store in stores:
        store.start()
    for store in stores:
        store.wait()


def on_device(right_side, initial_guess, v_factor, u_factor, tile_ranks, diag_block, diag_inverse):
    any_space = pl.BlockSpec(memory_space=pl.ANY)
    tiles, count, part, width = v_factor.shape
    rhs_count = initial_guess.shape[0]
    shape = jax.ShapeDtypeStruct(initial_guess.shape, F32)
    result = pl.pallas_call(
        kernel,
        name="richardson",
        out_shape=pltpu.VMEM((2, rhs_count, width), F32),
        in_specs=[any_space] * 7,
        out_specs=pl.BlockSpec(memory_space=pltpu.VMEM),
        scratch_shapes=[
            pltpu.VMEM((rhs_count, width), F32),
            pltpu.VMEM((rhs_count, width), F32),
            pltpu.VMEM((tiles, count, part, width), F32),
            pltpu.VMEM((tiles, count * part, width), BF16),
            pltpu.VMEM((tiles, count * part, width), BF16),
            pltpu.VMEM((tiles, count, part, width), F32),
            pltpu.VMEM((tiles, width, count * part), BF16),
            pltpu.VMEM((tiles, width, count * part), BF16),
            pltpu.VMEM((width, width), F32),
            pltpu.VMEM((width, width), BF16),
            pltpu.VMEM((width, width), BF16),
            pltpu.VMEM((width, width), F32),
            pltpu.VMEM((width, width), BF16),
            pltpu.VMEM((width, width), BF16),
            pltpu.VMEM((2, width, CHUNK), F32),
            pltpu.VMEM((2, 2, width, CHUNK), F32),
            pltpu.VMEM((2, 2, width, CHUNK), F32),
            pltpu.VMEM((2, width, CHUNK), F32),
            pltpu.VMEM((4, width, CHUNK), F32),
            pltpu.VMEM((4, width, CHUNK), F32),
            pltpu.VMEM((2, width, CHUNK), F32),
            pltpu.VMEM((4, 64, tiles, tiles, part, CHUNK), F32),
            pltpu.VMEM((4, 64, tiles, tiles, part, CHUNK), F32),
            pltpu.VMEM((1024, 2 * CHUNK), BF16),
            pltpu.VMEM((LATE, tiles, part, width), F32),
            pltpu.VMEM((width, LATE * tiles * part), BF16),
            pltpu.VMEM((width, LATE * tiles * part), BF16),
            pltpu.VMEM((2, LATE, tiles, part, CHUNK), F32),
            pltpu.SMEM(tile_ranks.shape[::-1], jnp.int32),
            pltpu.SMEM((64,), jnp.int32),
            pltpu.SMEM((64,), jnp.int32),
            pltpu.SemaphoreType.DMA((8,)),
            pltpu.SemaphoreType.DMA((4,)),
            pltpu.SemaphoreType.DMA((4, 2)),
            pltpu.SemaphoreType.DMA((4,)),
            pltpu.SemaphoreType.DMA((4,)),
            pltpu.SemaphoreType.DMA((4,)),
            pltpu.SemaphoreType.DMA((4,)),
            pltpu.SemaphoreType.DMA,
            pltpu.SemaphoreType.DMA,
            pltpu.SemaphoreType.DMA((2,)),
        ],
        compiler_params=pltpu.CompilerParams(
            collective_id=0, has_side_effects=True, vmem_limit_bytes=58 << 20
        ),
    )(right_side, initial_guess, v_factor, u_factor, tile_ranks.T, diag_block, diag_inverse)
    return pl.pallas_call(
        finish,
        name="finish",
        out_shape=(shape, shape),
        in_specs=[pl.BlockSpec(memory_space=pltpu.VMEM)],
        out_specs=(any_space, any_space),
        scratch_shapes=[pltpu.SemaphoreType.DMA((2,))],
        compiler_params=pltpu.CompilerParams(vmem_limit_bytes=8 << 20),
    )(result)


def solution(mesh):
    placed = (
        P(None, "row"),
        P(None, ("row", "pan")),
        P("row", None, "pan", None),
        P("row", None, "pan", None),
        P(None, "row"),
        P(("row", "pan"), None),
        P(("row", "pan"), None),
    )
    return jax.shard_map(
        on_device,
        mesh=mesh,
        in_specs=placed,
        out_specs=(P(None, ("row", "pan")), P(None, ("row", "pan"))),
        check_vma=False,
    )
```
